32 devices in a mesh: sp: 2 (over x), fsdp: 16 (over z, y, core).
Axes of the slice: x: 2, y: 2, z: 4, core: 2. Of those that a mesh axis runs over, the one named last changes fastest.
Arguments:
- tokens: bfloat16 [16, 1024, 1024], P('fsdp', 'sp'), may hold values from -6 to 6
- segments: int32 [16, 1024], P('fsdp', 'sp'), may hold values from 0 to 7, never falling along the last dimension, each value on 1 to 256 neighbouring positions
- cotangent: bfloat16 [16, 1024, 1024], P('fsdp', 'sp'), may hold values from -6 to 6
- gain_attn: bfloat16 [1024], P('fsdp'), may hold values from 0.5 to 1.5
- w_fac: bfloat16 [1024, 800], P('fsdp'), may hold values from -0.25 to 0.25
- w_out: bfloat16 [1024, 1024], P('fsdp'), may hold values from -0.75 to 0.75
- gain_ffn: bfloat16 [1024], P('fsdp'), may hold values from 0.5 to 1.5
- w_gu: bfloat16 [1024, 5632], P('fsdp'), may hold values from -0.1875 to 0.1875
- w_down: bfloat16 [2816, 1024], P('fsdp'), may hold values from -0.109375 to 0.109375
Outputs:
- out: bfloat16 [16, 1024, 1024], P('fsdp', 'sp')
- grad_tokens: float32 [16, 1024, 1024], P('fsdp', 'sp')
- grad_gain_attn: float32 [1024], P('fsdp')
- grad_w_fac: float32 [1024, 800], P('fsdp')
- grad_w_out: float32 [1024, 1024], P('fsdp')
- grad_gain_ffn: float32 [1024], P('fsdp')
- grad_w_gu: float32 [1024, 5632], P('fsdp')
- grad_w_down: float32 [2816, 1024], P('fsdp')
The draws below stay inside these ranges and needn't reach their ends.
Inputs may be any that keep to these rules, and one draw needn't show every extreme that they name: `segments`: each row of 1024 numbers never falls and uses all 8 document numbers; a document has at most 256 tokens, and one of each row has exactly that many.
All inputs are finite; a program needn't handle non-finite values.
Results may differ from the reference program's by a relative error of at most 0.023.
Values may be sent and summed in bfloat16 or wider, within the bound.
A program may use at most 192 MiB of HBM per device.

```python
import math
from functools import partial
import jax
import jax.numpy as jnp
import numpy as np
from jax import lax

D = 1024
H = 16
DH = 64
RQ = 6
RK = 2
FF = 2816
DOCS = 8
LEN = 1024
FAC = 800
N_FSDP = 16


def levels(stream_key, extent, pieces, low, largest):
    def one(dim, parts):
        steps = jax.random.uniform(jax.random.fold_in(jax.random.fold_in(stream_key, 6), dim), (parts,), jnp.float32, low / len(pieces), largest / len(pieces))
        return jnp.repeat(jnp.exp(steps), extent[dim] // parts).reshape((-1,) + (1,) * (len(extent) - dim - 1))

    factor_of = one(*pieces[0])
    for cut in pieces[1:]:
        factor_of = factor_of * one(*cut)
    return factor_of


def length_profile(count, total, limit, slope):
    loads = [(1 << 20) // math.isqrt(grade ** slope) + 1 for grade in range(2, count + 1)]
    rest, counts = total - limit - (count - 1), [1] * (count - 1)
    while rest > 0:
        movable = [i for i in range(count - 1) if counts[i] < limit]
        pool, budget = sum([loads[i] for i in movable]), rest
        for i in movable:
            more = min(limit - counts[i], max(1, budget * loads[i] // pool), rest)
            counts[i] = counts[i] + more
            rest = rest - more
    return np.array([limit] + counts)


def ragged_sizes(rng, amount, total, most, skew):
    if amount == 2:
        one = jax.random.randint(rng, (), max(1, total - most), min(most, total - 1) + 1)
        return jnp.stack([one, total - one])
    tallies = jnp.asarray(length_profile(amount, total, most, skew), jnp.int32)
    twos = (amount - 1) // 2
    giver, sink = tallies[1:1 + 2 * twos:2], tallies[2:2 + 2 * twos:2]
    room = jnp.minimum(giver - 1, most - sink)
    passed = jax.random.randint(jax.random.fold_in(rng, 1), (twos,), 0, 1 << 20) % (room + 1)
    tallies = tallies.at[1:1 + 2 * twos:2].set(giver - passed).at[2:2 + 2 * twos:2].set(sink + passed)
    return tallies[jax.random.permutation(jax.random.fold_in(rng, 2), amount)]


def scatter_about(key, shape, width, most, shards=(), kind=jnp.bfloat16):
    loudness = levels(key, shape, shards, -0.22, 0.18) if shards else 1.0
    drawn = jax.random.normal(key, shape, jnp.float32) * width * loudness
    return jnp.minimum(jnp.maximum(drawn, -most), most).astype(kind)


def setup_inputs(seed: int = 0) -> dict:
    key_list = jax.random.split(jax.random.key(seed), 10)
    tokens = scatter_about(key_list[0], (N_FSDP, LEN, D), 1.0, 6.0, ((0, 16), (1, 2)))
    segments = jax.vmap(lambda own: jnp.searchsorted(jnp.cumsum(ragged_sizes(own, DOCS, LEN, LEN // 4, 1)), jnp.arange(LEN), side="right"))(jax.random.split(key_list[1], N_FSDP)).reshape((N_FSDP, LEN)).astype(jnp.int32)
    cotangent = scatter_about(key_list[2], (N_FSDP, LEN, D), 1.0, 6.0, ((0, 16), (1, 2)))
    gain_attn = jnp.clip(1.0 + 0.1 * jax.random.normal(key_list[3], (D,), jnp.float32), 0.5, 1.5).astype(jnp.bfloat16)
    w_fac = scatter_about(key_list[4], (D, FAC), (D // 2) ** -0.5, 0.25, ((0, 16),))
    w_out = scatter_about(key_list[5], (H * DH, D), (H * DH // 16) ** -0.5, 0.75, ((0, 16),))
    gain_ffn = jnp.clip(1.0 + 0.1 * jax.random.normal(key_list[6], (D,), jnp.float32), 0.5, 1.5).astype(jnp.bfloat16)
    w_gu = scatter_about(key_list[7], (D, 2 * FF), D ** -0.5, 0.1875, ((0, 16),))
    w_down = scatter_about(key_list[8], (FF, D), FF ** -0.5, 0.109375, ((0, 16),))
    return {"tokens": tokens, "segments": segments, "cotangent": cotangent, "gain_attn": gain_attn, "w_fac": w_fac, "w_out": w_out, "gain_ffn": gain_ffn, "w_gu": w_gu, "w_down": w_down}


EPSILON = 1e-06
PRECISE = lax.Precision.HIGHEST

@jax.custom_vjp
def low(v):
    return lax.optimization_barrier(v.astype(jnp.bfloat16)).astype(jnp.float32)

@jax.custom_vjp
def low_back(v):
    return v

def low_keep(v):
    return (low(v), None)

def low_pass(kept, grad):
    return (grad,)

def back_keep(v):
    return (v, None)

def back_low(kept, grad):
    return (low(grad),)
low.defvjp(low_keep, low_pass)
low_back.defvjp(back_keep, back_low)

def rms_norm(values, gain_row):
    factor = lax.rsqrt(lax.optimization_barrier(jnp.mean(values * values, axis=-1, keepdims=True)) + EPSILON)
    return values * factor * gain_row

def dense(left, right):
    return jnp.dot(left, right, precision=PRECISE, preferred_element_type=jnp.float32)

def build_heads(factor_rows):
    token_count = factor_rows.shape[0]
    span_query = H * RQ
    span_kv = H * RK
    query_left = factor_rows[:, :span_query].reshape(token_count, H, RQ)
    key_left = factor_rows[:, span_query:span_query + span_kv].reshape(token_count, H, RK)
    value_left = factor_rows[:, span_query + span_kv:span_query + 2 * span_kv].reshape(token_count, H, RK)
    offset = span_query + 2 * span_kv
    query_right = factor_rows[:, offset:offset + RQ * DH].reshape(token_count, RQ, DH)
    key_right = factor_rows[:, offset + RQ * DH:offset + (RQ + RK) * DH].reshape(token_count, RK, DH)
    value_right = factor_rows[:, offset + (RQ + RK) * DH:offset + (RQ + 2 * RK) * DH].reshape(token_count, RK, DH)
    queries = jnp.einsum('thr,trd->thd', query_left, query_right, precision=PRECISE) / RQ
    keys_built = jnp.einsum('thr,trd->thd', key_left, key_right, precision=PRECISE) / RK
    values_built = jnp.einsum('thr,trd->thd', value_left, value_right, precision=PRECISE) / RK
    return (queries.reshape(token_count, H * DH), keys_built.reshape(token_count, H * DH), values_built.reshape(token_count, H * DH))

def attend(queries, keys_all, values_all, seg_all):
    block_rows = min(512, LEN)
    key_heads = keys_all.reshape(LEN, H, DH)
    value_heads = values_all.reshape(LEN, H, DH)
    key_positions = jnp.arange(LEN, dtype=jnp.int32)

    def one_block(block_index):
        offset = (block_index * block_rows).astype(jnp.int32)
        query_block = lax.dynamic_slice_in_dim(queries, offset, block_rows, 0).reshape(block_rows, H, DH)
        seg_block = lax.dynamic_slice_in_dim(seg_all, offset, block_rows, 0)
        logits = jnp.einsum('qhd,khd->hqk', query_block, key_heads, precision=PRECISE) * DH ** (-0.5)
        logits = low_back(logits)
        positions = offset + jnp.arange(block_rows, dtype=jnp.int32)
        allowed = (seg_block[:, None] == seg_all[None, :]) & (key_positions[None, :] <= positions[:, None])
        logits = jnp.where(allowed[None], logits, -1e+30)
        row_peak = lax.optimization_barrier(jnp.max(logits, axis=-1, keepdims=True))
        exponent = jnp.exp(logits - row_peak)
        weights = low(exponent / lax.optimization_barrier(jnp.sum(exponent, axis=-1, keepdims=True)))
        mixed_block = jnp.einsum('hqk,khd->qhd', weights, value_heads, precision=PRECISE)
        return mixed_block.reshape(block_rows, H * DH)
    mixed_all = lax.map(jax.checkpoint(one_block), jnp.arange(LEN // block_rows, dtype=jnp.int32))
    return mixed_all.reshape(LEN, H * DH)

def per_sequence(packed):
    return attend(packed[0], packed[1], packed[2], packed[3])

def forward(tokens, gain_attn, w_fac, w_out, gain_ffn, w_gu, w_down, segments):
    flat_tokens = tokens.reshape(-1, D)
    normed_one = low(rms_norm(flat_tokens, gain_attn))
    factor_rows = low_back(dense(normed_one, w_fac))
    queries, keys_built, values_built = build_heads(factor_rows)
    queries = low(low_back(queries))
    keys_built = low(low_back(keys_built))
    values_built = low(low_back(values_built))
    attended = lax.map(per_sequence, (queries.reshape(N_FSDP, LEN, H * DH), keys_built.reshape(N_FSDP, LEN, H * DH), values_built.reshape(N_FSDP, LEN, H * DH), segments))
    attended = low(low_back(attended.reshape(-1, H * DH)))
    branch = low_back(dense(attended, w_out))
    hidden_in = flat_tokens + branch
    normed_two = low(rms_norm(hidden_in, gain_ffn))
    gate_up = low_back(dense(normed_two, w_gu))
    activated = low(jax.nn.silu(gate_up[:, :FF]) * gate_up[:, FF:])
    ffn_out = low_back(dense(activated, w_down))
    return (hidden_in + ffn_out).reshape(tokens.shape)

def reference(tokens, segments, cotangent, gain_attn, w_fac, w_out, gain_ffn, w_gu, w_down):
    result, pull_back = jax.vjp(partial(forward, segments=segments), tokens.astype(jnp.float32), gain_attn.astype(jnp.float32), w_fac.astype(jnp.float32), w_out.astype(jnp.float32), gain_ffn.astype(jnp.float32), w_gu.astype(jnp.float32), w_down.astype(jnp.float32))
    gradients = pull_back(cotangent.astype(jnp.float32))
    return (result.astype(jnp.bfloat16), gradients[0], gradients[1], gradients[2], gradients[3], gradients[4], gradients[5], gradients[6])
```

```python
import functools

import jax
import jax.numpy as jnp
from jax import lax
from jax.experimental import pallas as pl
from jax.experimental.pallas import tpu as pltpu
from jax.sharding import PartitionSpec as P

H = 16
DH = 64
RQ = 6
RK = 2
FF = 2816
LANES = 128
NB = (RQ + 2 * RK) * DH
RANKS = RQ + 2 * RK

EPSILON = 1e-06
NEG = -1e30
F32 = jnp.float32
BF16 = jnp.bfloat16


def rms_norm(values, gain_row):
    factor = lax.rsqrt(jnp.mean(values * values, axis=-1, keepdims=True) + EPSILON)
    return values * factor * gain_row


def swiglu(gate_up):
    return jax.nn.silu(gate_up[:, :FF]) * gate_up[:, FF:]


def product(left, right):
    return jnp.dot(left, right, preferred_element_type=F32)


def weight_grad(left, right):
    return jnp.einsum("ta,tb->ab", left, right, preferred_element_type=F32)


def back_product(grad_rows, weight):
    return jnp.einsum("tb,ab->ta", grad_rows, weight, preferred_element_type=F32)


def dot_nt(a, b):
    return lax.dot_general(a, b, (((1,), (1,)), ((), ())), preferred_element_type=F32)


def dot_tn(a, b):
    return lax.dot_general(a, b, (((0,), (0,)), ((), ())), preferred_element_type=F32)


def band_start(index, block, width):
    return pl.multiple_of(jnp.maximum(index * block - (width - block), 0), LANES)


def band_bias(index, start, seg_col, seg_row, block, width):
    rows = index * block + lax.broadcasted_iota(jnp.int32, (block, width), 0)
    cols = start + lax.broadcasted_iota(jnp.int32, (block, width), 1)
    keep = (seg_col == seg_row) & (cols <= rows)
    return jnp.where(keep, 0.0, NEG)


def half_masks(scale):
    lane = lax.broadcasted_iota(jnp.int32, (1, LANES), 1)
    low = jnp.where(lane < DH, scale, 0.0).astype(BF16)
    high = jnp.where(lane < DH, 0.0, scale).astype(BF16)
    return low, high


def split_pair(values, masks):
    return jnp.concatenate([values * masks[0], values * masks[1]], axis=0)


def attend_forward_kernel(q_ref, k_ref, v_ref, segc_ref, segr_ref, o_ref, *, block, width):
    index = pl.program_id(0)
    start = band_start(index, block, width)
    bias = band_bias(index, start, segc_ref[...], segr_ref[:, pl.ds(start, width)], block, width)
    bias = jnp.concatenate([bias, bias], axis=0)
    masks = half_masks(DH ** (-0.5))
    first = lax.broadcasted_iota(jnp.int32, (block, LANES), 1) < DH
    for pair in range(q_ref.shape[1] // LANES):
        lanes = slice(pair * LANES, (pair + 1) * LANES)
        queries = split_pair(q_ref[:, lanes], masks)
        keys = k_ref[pl.ds(start, width), lanes]
        values = v_ref[pl.ds(start, width), lanes]
        scores = dot_nt(queries, keys) + bias
        exponent = jnp.exp(scores - jnp.max(scores, axis=-1, keepdims=True))
        inverse = 1.0 / jnp.sum(exponent, axis=-1, keepdims=True)
        probs = (exponent * inverse).astype(BF16)
        mixed = product(probs, values)
        o_ref[:, lanes] = jnp.where(first, mixed[:block], mixed[block:]).astype(BF16)


def attend_backward_kernel(
    q_ref, k_ref, v_ref, g_ref, segc_ref, segr_ref, dq_ref, dk_ref, dv_ref, dk_acc, dv_acc,
    *, block, width
):
    index = pl.program_id(0)
    start = band_start(index, block, width)
    scaling = DH ** (-0.5)

    @pl.when(index == 0)
    def _():
        dk_acc[...] = jnp.zeros_like(dk_acc)
        dv_acc[...] = jnp.zeros_like(dv_acc)

    bias = band_bias(index, start, segc_ref[...], segr_ref[:, pl.ds(start, width)], block, width)
    bias = jnp.concatenate([bias, bias], axis=0)
    scale_masks = half_masks(scaling)
    unit_masks = half_masks(1.0)
    first = lax.broadcasted_iota(jnp.int32, (block, LANES), 1) < DH
    window = pl.ds(start, width)
    for pair in range(q_ref.shape[1] // LANES):
        lanes = slice(pair * LANES, (pair + 1) * LANES)
        queries = split_pair(q_ref[:, lanes], scale_masks)
        grads = split_pair(g_ref[:, lanes], unit_masks)
        keys = k_ref[window, lanes]
        values = v_ref[window, lanes]
        scores = dot_nt(queries, keys) + bias
        exponent = jnp.exp(scores - jnp.max(scores, axis=-1, keepdims=True))
        inverse = 1.0 / jnp.sum(exponent, axis=-1, keepdims=True)
        probs = exponent * inverse
        grad_probs = dot_nt(grads, values)
        inner = jnp.sum(probs * grad_probs, axis=-1, keepdims=True)
        grad_scores = (probs * (grad_probs - inner)).astype(BF16)
        grad_q = product(grad_scores, keys) * scaling
        dq_ref[:, lanes] = jnp.where(first, grad_q[:block], grad_q[block:]).astype(BF16)
        dk_acc[window, lanes] += dot_tn(grad_scores, queries)
        dv_acc[window, lanes] += dot_tn(probs.astype(BF16), grads)

    @pl.when(index == pl.num_programs(0) - 1)
    def _():
        dk_ref[...] = dk_acc[...].astype(BF16)
        dv_ref[...] = dv_acc[...].astype(BF16)


def attention_specs(length, columns):
    block = LANES
    width = min(length // 4 + block, length)
    whole = pl.BlockSpec((length, columns), lambda i: (0, 0))
    rows = pl.BlockSpec((block, columns), lambda i: (i, 0))
    seg_col = pl.BlockSpec((block, 1), lambda i: (i, 0))
    seg_row = pl.BlockSpec((1, length), lambda i: (0, 0))
    return block, width, whole, rows, seg_col, seg_row


def attend_forward(queries, keys, values, seg_all):
    length, columns = queries.shape
    block, width, whole, rows, seg_col, seg_row = attention_specs(length, columns)
    work = length * width * columns
    return pl.pallas_call(
        functools.partial(attend_forward_kernel, block=block, width=width),
        grid=(length // block,),
        in_specs=[rows, whole, whole, seg_col, seg_row],
        out_specs=rows,
        out_shape=jax.ShapeDtypeStruct((length, columns), BF16),
        cost_estimate=pl.CostEstimate(
            flops=16 * work, bytes_accessed=8 * length * columns, transcendentals=work // DH
        ),
        name="attend_forward",
    )(queries, keys, values, seg_all.reshape(length, 1), seg_all.reshape(1, length))


def attend_backward(queries, keys, values, grads, seg_all):
    length, columns = queries.shape
    block, width, whole, rows, seg_col, seg_row = attention_specs(length, columns)
    work = length * width * columns
    shape = jax.ShapeDtypeStruct((length, columns), BF16)
    return pl.pallas_call(
        functools.partial(attend_backward_kernel, block=block, width=width),
        grid=(length // block,),
        in_specs=[rows, whole, whole, rows, seg_col, seg_row],
        out_specs=[rows, whole, whole],
        out_shape=[shape, shape, shape],
        scratch_shapes=[pltpu.VMEM((length, columns), F32), pltpu.VMEM((length, columns), F32)],
        cost_estimate=pl.CostEstimate(
            flops=40 * work, bytes_accessed=14 * length * columns, transcendentals=work // DH
        ),
        name="attend_backward",
    )(queries, keys, values, grads, seg_all.reshape(length, 1), seg_all.reshape(1, length))


def expansion(heads):
    rows = lax.broadcasted_iota(jnp.int32, (2 * LANES, RANKS * heads * DH), 0) % LANES
    cols = lax.broadcasted_iota(jnp.int32, (2 * LANES, RANKS * heads * DH), 1)
    rank, head = cols // (heads * DH), (cols % (heads * DH)) // DH
    in_k = heads * RQ + head * RK + rank - RQ
    in_v = heads * (RQ + RK) + head * RK + rank - RQ - RK
    source = jnp.where(
        rank < RQ, head * RQ + rank, jnp.where(rank < RQ + RK, in_k, in_v)
    )
    return (rows == source).astype(BF16)


def high_low(values):
    high = values.astype(BF16)
    return high, (values - high.astype(F32)).astype(BF16)


def doubled(factor, rank, first):
    pair = factor[:, (rank // 2) * LANES : (rank // 2 + 1) * LANES]
    turned = pltpu.roll(pair, DH, 1)
    return jnp.where(first, pair, turned) if rank % 2 == 0 else jnp.where(first, turned, pair)


GROUPS = ((0, RQ), (RQ, RK), (RQ + RK, RK))


def heads_forward_kernel(x_ref, gain_ref, w_ref, e_ref, f_ref, q_ref, k_ref, v_ref):
    normed = rms_norm(x_ref[...].astype(F32), gain_ref[...]).astype(BF16)
    factor = product(normed, w_ref[...])
    f_ref[...] = factor
    spread = jnp.concatenate(high_low(factor[:, NB:]), axis=1)
    rows, columns = q_ref.shape
    first = lax.broadcasted_iota(jnp.int32, (rows, LANES), 1) < DH
    for (base, ranks), out_ref in zip(GROUPS, (q_ref, k_ref, v_ref)):
        total = None
        for rank in range(base, base + ranks):
            left = product(spread, e_ref[:, rank * columns : (rank + 1) * columns])
            right = jnp.concatenate([doubled(factor, rank, first)] * (columns // LANES), axis=1)
            total = left * right if total is None else total + left * right
        out_ref[...] = (total * (1.0 / ranks)).astype(BF16)


def heads_backward_kernel(f_ref, e_ref, dq_ref, dk_ref, dv_ref, g_ref):
    factor = f_ref[...]
    spread = jnp.concatenate(high_low(factor[:, NB:]), axis=1)
    rows, columns = dq_ref.shape
    first = lax.broadcasted_iota(jnp.int32, (rows, LANES), 1) < DH
    left_total = jnp.zeros((rows, LANES), F32)
    folded = []
    for (base, ranks), grad_ref in zip(GROUPS, (dq_ref, dk_ref, dv_ref)):
        grad = grad_ref[...].astype(F32) * (1.0 / ranks)
        for rank in range(base, base + ranks):
            ones = e_ref[:, rank * columns : (rank + 1) * columns]
            weighted = product(spread, ones) * grad
            right_grad = weighted[:, :LANES]
            for chunk in range(1, columns // LANES):
                right_grad = right_grad + weighted[:, chunk * LANES : (chunk + 1) * LANES]
            folded.append(right_grad + pltpu.roll(right_grad, DH, 1))
            right = jnp.concatenate([doubled(factor, rank, first)] * (columns // LANES), axis=1)
            high, low = high_low(grad * right)
            left_total = left_total + dot_nt(high, ones[:LANES]) + dot_nt(low, ones[:LANES])
    for pair in range(RANKS // 2):
        g_ref[:, pair * LANES : (pair + 1) * LANES] = jnp.where(
            first, folded[2 * pair], folded[2 * pair + 1]
        ).astype(BF16)
    g_ref[:, NB:] = left_total.astype(BF16)


HEAD_ROWS = 256


def heads_forward(tokens, gain_row, weights, spreader, columns):
    length, width = tokens.shape
    rows = min(HEAD_ROWS, length)
    block = lambda n: pl.BlockSpec((rows, n), lambda i: (i, 0))
    fixed = lambda a: pl.BlockSpec(a.shape, lambda i: (0, 0))
    head = jax.ShapeDtypeStruct((length, columns), BF16)
    return pl.pallas_call(
        heads_forward_kernel,
        grid=(length // rows,),
        in_specs=[block(width), fixed(gain_row), fixed(weights), fixed(spreader)],
        out_specs=[block(NB + LANES)] + [block(columns)] * 3,
        out_shape=[jax.ShapeDtypeStruct((length, NB + LANES), F32), head, head, head],
        name="heads_forward",
    )(tokens, gain_row, weights, spreader)


def heads_backward(factors, spreader, grad_q, grad_k, grad_v):
    length, columns = grad_q.shape
    rows = min(HEAD_ROWS, length)
    block = lambda n: pl.BlockSpec((rows, n), lambda i: (i, 0))
    return pl.pallas_call(
        heads_backward_kernel,
        grid=(length // rows,),
        in_specs=[
            block(NB + LANES), pl.BlockSpec(spreader.shape, lambda i: (0, 0)),
            block(columns), block(columns), block(columns),
        ],
        out_specs=block(NB + LANES),
        out_shape=jax.ShapeDtypeStruct((length, NB + LANES), BF16),
        name="heads_backward",
    )(factors, spreader, grad_q, grad_k, grad_v)


def gather_shards(values, shards):
    me = lax.axis_index("sp")
    rows = values.shape[0]
    full = jnp.zeros((rows * shards,) + values.shape[1:], values.dtype)
    zeros = (0,) * (values.ndim - 1)
    full = lax.dynamic_update_slice(full, values, (me * rows,) + zeros)
    for shift in range(1, shards):
        part = lax.ppermute(values, "sp", [(i, (i + shift) % shards) for i in range(shards)])
        full = lax.dynamic_update_slice(full, part, (((me - shift) % shards) * rows,) + zeros)
    return full


def sum_shards(values, shards):
    if shards == 2:
        other = lax.ppermute(values, "sp", [(0, 1), (1, 0)])
        return values.astype(F32) + other.astype(F32)
    return lax.psum(values, "sp").astype(F32)


def arrange_factor(w, shards):
    heads = H // shards
    spans = ((0, RQ), (H * RQ, RK), (H * (RQ + RK), RK))
    parts = [w[:, H * RANKS :]]
    for device in range(shards):
        own = [
            w[:, base + device * heads * r : base + (device + 1) * heads * r] for base, r in spans
        ]
        parts.append(jnp.pad(jnp.concatenate(own, axis=1), ((0, 0), (0, LANES - heads * RANKS))))
    return jnp.concatenate(parts, axis=1)


def restore_factor(g, shards):
    heads = H // shards
    spans = ((0, RQ), (heads * RQ, RK), (heads * (RQ + RK), RK))
    parts = []
    for base, r in spans:
        for device in range(shards):
            begin = NB + device * LANES + base
            parts.append(g[:, begin : begin + heads * r])
    parts.append(g[:, :NB])
    return jnp.concatenate(parts, axis=1)


def local(tokens, segments, cotangent, gain_attn, w_fac, w_out, gain_ffn, w_gu, w_down, shards):
    me = lax.axis_index("sp")
    features = tokens.shape[2]
    heads = H // shards
    columns = heads * DH
    fac_columns = NB + shards * LANES
    own_rows = w_fac.shape[0]

    gains = jnp.stack([gain_attn, gain_ffn], axis=1)
    gains = jnp.pad(gains, ((0, 0), (0, LANES - 2)))
    packed = jnp.concatenate([arrange_factor(w_fac, shards), w_out, gains], axis=1)
    packed = lax.all_gather(packed, "fsdp", axis=0, tiled=True)
    gu_full = lax.all_gather(w_gu, "fsdp", axis=0, tiled=True)
    down_full = lax.all_gather(w_down, "fsdp", axis=0, tiled=True)
    fac_full = packed[:, :fac_columns]
    out_full = packed[:, fac_columns : fac_columns + features]
    gain_one = packed[:, fac_columns + features].astype(F32).reshape(1, -1)
    gain_two = packed[:, fac_columns + features + 1].astype(F32).reshape(1, -1)

    tokens_all = gather_shards(tokens[0], shards)
    seg_all = gather_shards(segments[0], shards)
    length = tokens_all.shape[0]
    own_left = lax.dynamic_slice_in_dim(fac_full, NB + me * LANES, LANES, 1)
    own_weights = jnp.concatenate([fac_full[:, :NB], own_left], axis=1)
    spreader = expansion(heads)
    factors, query_heads, key_heads, value_heads = heads_forward(
        tokens_all, gain_one, own_weights, spreader, columns
    )
    mixed_heads = attend_forward(query_heads, key_heads, value_heads, seg_all)
    mixed_tokens = lax.all_to_all(mixed_heads, "sp", split_axis=0, concat_axis=1, tiled=True)

    inputs = tokens[0].astype(F32)
    token_count = inputs.shape[0]
    hidden_in = inputs + product(mixed_tokens, out_full)
    normed_two = rms_norm(hidden_in, gain_two).astype(BF16)
    gate_up = product(normed_two, gu_full)
    activated = swiglu(gate_up).astype(BF16)
    grad_out = cotangent[0].astype(F32)
    grad_low = cotangent[0]
    grad_down = weight_grad(activated, grad_low).astype(BF16)
    grad_down = lax.psum_scatter(grad_down, "fsdp", scatter_dimension=0, tiled=True)

    result = hidden_in + product(activated, down_full)
    output = result.astype(BF16)[None]

    grad_act = back_product(grad_low, down_full)
    primal_ffn, pull_ffn = jax.vjp(swiglu, gate_up)
    grad_gate_up = pull_ffn(grad_act)[0].astype(BF16)
    grad_gu = weight_grad(normed_two, grad_gate_up).astype(BF16)
    grad_gate_up, grad_gu = lax.optimization_barrier((grad_gate_up, grad_gu))
    grad_gu = lax.psum_scatter(grad_gu, "fsdp", scatter_dimension=0, tiled=True)
    grad_normed_two = back_product(grad_gate_up, gu_full)
    primal_two, pull_two = jax.vjp(rms_norm, hidden_in, gain_two)
    grad_from_norm, grad_gain_two = pull_two(grad_normed_two)
    grad_hidden = grad_out + grad_from_norm
    grad_branch = grad_hidden.astype(BF16)
    grad_wout = weight_grad(mixed_tokens, grad_branch)
    grad_mixed = back_product(grad_branch, out_full).astype(BF16)
    grad_heads = lax.all_to_all(grad_mixed, "sp", split_axis=1, concat_axis=0, tiled=True)
    grad_q, grad_k, grad_v = attend_backward(
        query_heads, key_heads, value_heads, grad_heads, seg_all
    )
    grad_parts = heads_backward(factors, spreader, grad_q, grad_k, grad_v)
    grad_parts = lax.all_to_all(
        grad_parts.reshape(shards, token_count, NB + LANES), "sp", split_axis=0, concat_axis=0
    )
    grad_right = jnp.sum(grad_parts[:, :, :NB].astype(F32), axis=0).astype(BF16)
    grad_factor = jnp.concatenate(
        [grad_right] + [grad_parts[device, :, NB:] for device in range(shards)], axis=1
    )
    normed_one = rms_norm(inputs, gain_one).astype(BF16)
    grad_fac = weight_grad(normed_one, grad_factor)
    grad_normed_one = back_product(grad_factor, fac_full)
    primal_one, pull_one = jax.vjp(rms_norm, inputs, gain_one)
    grad_in_norm, grad_gain_one = pull_one(grad_normed_one)
    grad_tokens = (grad_hidden + grad_in_norm).reshape(1, token_count, features)

    grad_gains = jnp.concatenate([grad_gain_one, grad_gain_two], axis=0).T
    grad_gains = jnp.pad(grad_gains, ((0, 0), (0, LANES - 2)))
    grad_packed = jnp.concatenate(
        [grad_fac.astype(BF16), grad_wout.astype(BF16), grad_gains.astype(BF16)], axis=1
    )
    grad_packed = lax.psum_scatter(grad_packed, "fsdp", scatter_dimension=0, tiled=True)
    grad_down = sum_shards(grad_down, shards)
    grad_gu = sum_shards(grad_gu, shards)
    grad_packed = sum_shards(grad_packed, shards)
    return (
        output,
        grad_tokens,
        grad_packed[:, fac_columns + features],
        restore_factor(grad_packed[:, :fac_columns], shards),
        grad_packed[:, fac_columns : fac_columns + features],
        grad_packed[:, fac_columns + features + 1],
        grad_gu,
        grad_down,
    )


def solution(mesh):
    in_specs = (
        P("fsdp", "sp", None),
        P("fsdp", "sp"),
        P("fsdp", "sp", None),
        P("fsdp"),
        P("fsdp", None),
        P("fsdp", None),
        P("fsdp"),
        P("fsdp", None),
        P("fsdp", None),
    )
    out_specs = (
        P("fsdp", "sp", None),
        P("fsdp", "sp", None),
        P("fsdp"),
        P("fsdp", None),
        P("fsdp", None),
        P("fsdp"),
        P("fsdp", None),
        P("fsdp", None),
    )
    body = functools.partial(local, shards=mesh.shape["sp"])
    return jax.shard_map(body, mesh=mesh, in_specs=in_specs, out_specs=out_specs, check_vma=False)
```

```python
import functools

import jax
import jax.numpy as jnp
from jax import lax
from jax.experimental import pallas as pl
from jax.experimental.pallas import tpu as pltpu
from jax.sharding import PartitionSpec as P


H = 16
DH = 64
RQ = 6
RK = 2
FF = 2816
LANES = 128
NB = (RQ + 2 * RK) * DH
RANKS = RQ + 2 * RK

EPSILON = 1e-06
NEG = -1e30
F32 = jnp.float32
BF16 = jnp.bfloat16


def rms_norm(values, gain_row):
    factor = lax.rsqrt(jnp.mean(values * values, axis=-1, keepdims=True) + EPSILON)
    return values * factor * gain_row


def swiglu(gate_up):
    return jax.nn.silu(gate_up[:, :FF]) * gate_up[:, FF:]


def product(left, right):
    return jnp.dot(left, right, preferred_element_type=F32)


def weight_grad(left, right):
    return jnp.einsum("ta,tb->ab", left, right, preferred_element_type=F32)


def back_product(grad_rows, weight):
    return jnp.einsum("tb,ab->ta", grad_rows, weight, preferred_element_type=F32)


def dot_nt(a, b):
    return lax.dot_general(a, b, (((1,), (1,)), ((), ())), preferred_element_type=F32)


def dot_tn(a, b):
    return lax.dot_general(a, b, (((0,), (0,)), ((), ())), preferred_element_type=F32)


def band_start(index, block, width):
    return pl.multiple_of(jnp.maximum(index * block - (width - block), 0), LANES)


def band_bias(index, start, seg_col, seg_row, block, width):
    rows = index * block + lax.broadcasted_iota(jnp.int32, (block, width), 0)
    cols = start + lax.broadcasted_iota(jnp.int32, (block, width), 1)
    keep = (seg_col == seg_row) & (cols <= rows)
    return jnp.where(keep, 0.0, NEG)


def half_masks(scale):
    lane = lax.broadcasted_iota(jnp.int32, (1, LANES), 1)
    low = jnp.where(lane < DH, scale, 0.0).astype(BF16)
    high = jnp.where(lane < DH, 0.0, scale).astype(BF16)
    return low, high


def split_pair(values, masks):
    return jnp.concatenate([values * masks[0], values * masks[1]], axis=0)


def attend_forward_kernel(q_ref, k_ref, v_ref, segc_ref, segr_ref, o_ref, *, block, width):
    index = pl.program_id(0)
    start = band_start(index, block, width)
    bias = band_bias(index, start, segc_ref[...], segr_ref[:, pl.ds(start, width)], block, width)
    bias = jnp.concatenate([bias, bias], axis=0)
    masks = half_masks(DH ** (-0.5))
    first = lax.broadcasted_iota(jnp.int32, (block, LANES), 1) < DH
    for pair in range(q_ref.shape[1] // LANES):
        lanes = slice(pair * LANES, (pair + 1) * LANES)
        queries = split_pair(q_ref[:, lanes], masks)
        keys = k_ref[pl.ds(start, width), lanes]
        values = v_ref[pl.ds(start, width), lanes]
        scores = dot_nt(queries, keys) + bias
        exponent = jnp.exp(scores - jnp.max(scores, axis=-1, keepdims=True))
        inverse = 1.0 / jnp.sum(exponent, axis=-1, keepdims=True)
        probs = (exponent * inverse).astype(BF16)
        mixed = product(probs, values)
        o_ref[:, lanes] = jnp.where(first, mixed[:block], mixed[block:]).astype(BF16)


def attend_backward_kernel(
    q_ref, k_ref, v_ref, g_ref, segc_ref, segr_ref, dq_ref, dk_ref, dv_ref, dk_acc, dv_acc,
    *, block, width
):
    index = pl.program_id(0)
    start = band_start(index, block, width)
    scaling = DH ** (-0.5)

    @pl.when(index == 0)
    def _():
        dk_acc[...] = jnp.zeros_like(dk_acc)
        dv_acc[...] = jnp.zeros_like(dv_acc)

    bias = band_bias(index, start, segc_ref[...], segr_ref[:, pl.ds(start, width)], block, width)
    bias = jnp.concatenate([bias, bias], axis=0)
    scale_masks = half_masks(scaling)
    unit_masks = half_masks(1.0)
    first = lax.broadcasted_iota(jnp.int32, (block, LANES), 1) < DH
    window = pl.ds(start, width)
    for pair in range(q_ref.shape[1] // LANES):
        lanes = slice(pair * LANES, (pair + 1) * LANES)
        queries = split_pair(q_ref[:, lanes], scale_masks)
        grads = split_pair(g_ref[:, lanes], unit_masks)
        keys = k_ref[window, lanes]
        values = v_ref[window, lanes]
        scores = dot_nt(queries, keys) + bias
        exponent = jnp.exp(scores - jnp.max(scores, axis=-1, keepdims=True))
        inverse = 1.0 / jnp.sum(exponent, axis=-1, keepdims=True)
        probs = exponent * inverse
        grad_probs = dot_nt(grads, values)
        inner = jnp.sum(probs * grad_probs, axis=-1, keepdims=True)
        grad_scores = (probs * (grad_probs - inner)).astype(BF16)
        grad_q = product(grad_scores, keys) * scaling
        dq_ref[:, lanes] = jnp.where(first, grad_q[:block], grad_q[block:]).astype(BF16)
        dk_acc[window, lanes] += dot_tn(grad_scores, queries)
        dv_acc[window, lanes] += dot_tn(probs.astype(BF16), grads)

    @pl.when(index == pl.num_programs(0) - 1)
    def _():
        dk_ref[...] = dk_acc[...].astype(BF16)
        dv_ref[...] = dv_acc[...].astype(BF16)


def attention_specs(length, columns):
    block = LANES
    width = min(length // 4 + block, length)
    whole = pl.BlockSpec((length, columns), lambda i: (0, 0))
    rows = pl.BlockSpec((block, columns), lambda i: (i, 0))
    seg_col = pl.BlockSpec((block, 1), lambda i: (i, 0))
    seg_row = pl.BlockSpec((1, length), lambda i: (0, 0))
    return block, width, whole, rows, seg_col, seg_row


def attend_forward(queries, keys, values, seg_all):
    length, columns = queries.shape
    block, width, whole, rows, seg_col, seg_row = attention_specs(length, columns)
    work = length * width * columns
    return pl.pallas_call(
        functools.partial(attend_forward_kernel, block=block, width=width),
        grid=(length // block,),
        in_specs=[rows, whole, whole, seg_col, seg_row],
        out_specs=rows,
        out_shape=jax.ShapeDtypeStruct((length, columns), BF16),
        cost_estimate=pl.CostEstimate(
            flops=16 * work, bytes_accessed=8 * length * columns, transcendentals=work // DH
        ),
        name="attend_forward",
    )(queries, keys, values, seg_all.reshape(length, 1), seg_all.reshape(1, length))


def attend_backward(queries, keys, values, grads, seg_all):
    length, columns = queries.shape
    block, width, whole, rows, seg_col, seg_row = attention_specs(length, columns)
    work = length * width * columns
    shape = jax.ShapeDtypeStruct((length, columns), BF16)
    return pl.pallas_call(
        functools.partial(attend_backward_kernel, block=block, width=width),
        grid=(length // block,),
        in_specs=[rows, whole, whole, rows, seg_col, seg_row],
        out_specs=[rows, whole, whole],
        out_shape=[shape, shape, shape],
        scratch_shapes=[pltpu.VMEM((length, columns), F32), pltpu.VMEM((length, columns), F32)],
        cost_estimate=pl.CostEstimate(
            flops=40 * work, bytes_accessed=14 * length * columns, transcendentals=work // DH
        ),
        name="attend_backward",
    )(queries, keys, values, grads, seg_all.reshape(length, 1), seg_all.reshape(1, length))


def expansion(heads):
    rows = lax.broadcasted_iota(jnp.int32, (2 * LANES, RANKS * heads * DH), 0) % LANES
    cols = lax.broadcasted_iota(jnp.int32, (2 * LANES, RANKS * heads * DH), 1)
    rank, head = cols // (heads * DH), (cols % (heads * DH)) // DH
    in_k = heads * RQ + head * RK + rank - RQ
    in_v = heads * (RQ + RK) + head * RK + rank - RQ - RK
    source = jnp.where(
        rank < RQ, head * RQ + rank, jnp.where(rank < RQ + RK, in_k, in_v)
    )
    return (rows == source).astype(BF16)


def high_low(values):
    high = values.astype(BF16)
    return high, (values - high.astype(F32)).astype(BF16)


def doubled(factor, rank, first):
    pair = factor[:, (rank // 2) * LANES : (rank // 2 + 1) * LANES]
    turned = pltpu.roll(pair, DH, 1)
    return jnp.where(first, pair, turned) if rank % 2 == 0 else jnp.where(first, turned, pair)


GROUPS = ((0, RQ), (RQ, RK), (RQ + RK, RK))


def heads_forward_kernel(x_ref, gain_ref, w_ref, e_ref, f_ref, q_ref, k_ref, v_ref):
    normed = rms_norm(x_ref[...].astype(F32), gain_ref[...]).astype(BF16)
    factor = product(normed, w_ref[...])
    f_ref[...] = factor
    spread = jnp.concatenate(high_low(factor[:, NB:]), axis=1)
    rows, columns = q_ref.shape
    first = lax.broadcasted_iota(jnp.int32, (rows, LANES), 1) < DH
    for (base, ranks), out_ref in zip(GROUPS, (q_ref, k_ref, v_ref)):
        total = None
        for rank in range(base, base + ranks):
            left = product(spread, e_ref[:, rank * columns : (rank + 1) * columns])
            right = jnp.concatenate([doubled(factor, rank, first)] * (columns // LANES), axis=1)
            total = left * right if total is None else total + left * right
        out_ref[...] = (total * (1.0 / ranks)).astype(BF16)


def heads_backward_kernel(f_ref, e_ref, dq_ref, dk_ref, dv_ref, g_ref):
    factor = f_ref[...]
    spread = jnp.concatenate(high_low(factor[:, NB:]), axis=1)
    rows, columns = dq_ref.shape
    first = lax.broadcasted_iota(jnp.int32, (rows, LANES), 1) < DH
    left_total = jnp.zeros((rows, LANES), F32)
    folded = []
    for (base, ranks), grad_ref in zip(GROUPS, (dq_ref, dk_ref, dv_ref)):
        grad = grad_ref[...].astype(F32) * (1.0 / ranks)
        for rank in range(base, base + ranks):
            ones = e_ref[:, rank * columns : (rank + 1) * columns]
            weighted = product(spread, ones) * grad
            right_grad = weighted[:, :LANES]
            for chunk in range(1, columns // LANES):
                right_grad = right_grad + weighted[:, chunk * LANES : (chunk + 1) * LANES]
            folded.append(right_grad + pltpu.roll(right_grad, DH, 1))
            right = jnp.concatenate([doubled(factor, rank, first)] * (columns // LANES), axis=1)
            high, low = high_low(grad * right)
            left_total = left_total + dot_nt(high, ones[:LANES]) + dot_nt(low, ones[:LANES])
    for pair in range(RANKS // 2):
        g_ref[:, pair * LANES : (pair + 1) * LANES] = jnp.where(
            first, folded[2 * pair], folded[2 * pair + 1]
        ).astype(BF16)
    g_ref[:, NB:] = left_total.astype(BF16)


HEAD_ROWS = 256


def heads_forward(tokens, gain_row, weights, spreader, columns):
    length, width = tokens.shape
    rows = min(HEAD_ROWS, length)
    block = lambda n: pl.BlockSpec((rows, n), lambda i: (i, 0))
    fixed = lambda a: pl.BlockSpec(a.shape, lambda i: (0, 0))
    head = jax.ShapeDtypeStruct((length, columns), BF16)
    return pl.pallas_call(
        heads_forward_kernel,
        grid=(length // rows,),
        in_specs=[block(width), fixed(gain_row), fixed(weights), fixed(spreader)],
        out_specs=[block(NB + LANES)] + [block(columns)] * 3,
        out_shape=[jax.ShapeDtypeStruct((length, NB + LANES), F32), head, head, head],
        name="heads_forward",
    )(tokens, gain_row, weights, spreader)


def heads_backward(factors, spreader, grad_q, grad_k, grad_v):
    length, columns = grad_q.shape
    rows = min(HEAD_ROWS, length)
    block = lambda n: pl.BlockSpec((rows, n), lambda i: (i, 0))
    return pl.pallas_call(
        heads_backward_kernel,
        grid=(length // rows,),
        in_specs=[
            block(NB + LANES), pl.BlockSpec(spreader.shape, lambda i: (0, 0)),
            block(columns), block(columns), block(columns),
        ],
        out_specs=block(NB + LANES),
        out_shape=jax.ShapeDtypeStruct((length, NB + LANES), BF16),
        name="heads_backward",
    )(factors, spreader, grad_q, grad_k, grad_v)


MESH_ID = pl.DeviceIdType.MESH


def place(count):
    me = lax.axis_index("fsdp")
    line, side, core = me // 4, (me // 2) % 2, me % 2
    return me, line, side, core, count // 4


def spot(line, side, core):
    return (line * 2 + side) * 2 + core


def meet(peers):
    barrier = pltpu.get_barrier_semaphore()
    for peer in peers:
        pl.semaphore_signal(barrier, inc=1, device_id=peer, device_id_type=MESH_ID)
    pl.semaphore_wait(barrier, len(peers))


def gather_kernel(x_ref, o_ref, local_sem, send_sem, recv_sem, *, count):
    me, line, side, core, lines = place(count)
    across = [{"fsdp": spot(lax.rem(line + s, lines), side, core)} for s in range(1, lines)]
    beside, partner = {"fsdp": spot(line, 1 - side, core)}, {"fsdp": spot(line, side, 1 - core)}
    meet(across + [beside, partner])
    sends = []

    def copy(src, shard, slot, peer):
        return pltpu.make_async_remote_copy(
            src_ref=src, dst_ref=o_ref.at[shard], send_sem=send_sem.at[slot],
            recv_sem=recv_sem.at[shard], device_id=peer, device_id_type=MESH_ID,
        )

    def send(src, shard, peer):
        made = copy(src, shard, len(sends), peer)
        made.start()
        sends.append(made)

    def arrive(shard):
        copy(o_ref.at[shard], shard, 0, partner).wait_recv()

    own = pltpu.make_async_copy(x_ref, o_ref.at[me], local_sem)
    own.start()
    for peer in across:
        send(x_ref, me, peer)
    send(x_ref, me, beside)
    send(x_ref, me, partner)
    sources = [lax.rem(line + lines - s, lines) for s in range(1, lines)]
    for source in sources:
        shard = spot(source, side, core)
        arrive(shard)
        send(o_ref.at[shard], shard, beside)
        send(o_ref.at[shard], shard, partner)
    for source in [line] + sources:
        shard = spot(source, 1 - side, core)
        arrive(shard)
        send(o_ref.at[shard], shard, partner)
    for source in [line] + sources:
        arrive(spot(source, side, 1 - core))
        arrive(spot(source, 1 - side, 1 - core))
    own.wait()
    for made in sends:
        made.wait_send()


def gather_packed(values, count):
    lines = count // 4
    full = pl.pallas_call(
        functools.partial(gather_kernel, count=count),
        out_shape=jax.ShapeDtypeStruct((count,) + values.shape, values.dtype),
        in_specs=[pl.BlockSpec(memory_space=pltpu.VMEM)],
        out_specs=pl.BlockSpec(memory_space=pltpu.VMEM),
        scratch_shapes=[
            pltpu.SemaphoreType.DMA,
            pltpu.SemaphoreType.DMA((4 * lines - 1,)),
            pltpu.SemaphoreType.DMA((count,)),
        ],
        compiler_params=pltpu.CompilerParams(collective_id=0, has_side_effects=True),
        name="gather_packed",
    )(values)
    return full


def scatter_kernel(
    fac_ref, out_ref, gains_ref, o_ref, part, core_in, side_in, line_in, mine, sp_in,
    core_send, core_recv, side_send, side_recv, line_send, line_recv, sp_send, sp_recv,
    *, count, shards
):
    me, line, side, core, lines = place(count)
    rank = lax.axis_index("sp")
    rows = o_ref.shape[0]
    across = [{"fsdp": spot(lax.rem(line + s, lines), side, core)} for s in range(1, lines)]
    beside, partner = {"fsdp": spot(line, 1 - side, core)}, {"fsdp": spot(line, side, 1 - core)}
    others = [{"sp": lax.rem(rank + s, shards)} for s in range(1, shards)]
    meet(across + [beside, partner] + others)
    started = []

    def copy(src, dst, send_sem, recv_sem, peer):
        return pltpu.make_async_remote_copy(
            src_ref=src, dst_ref=dst, send_sem=send_sem, recv_sem=recv_sem,
            device_id=peer, device_id_type=MESH_ID,
        )

    def send(*args):
        made = copy(*args)
        made.start()
        started.append(made)

    def load(shard):
        begin = pl.multiple_of(shard * rows, rows)
        return jnp.concatenate(
            [fac_ref[pl.ds(begin, rows), :], out_ref[pl.ds(begin, rows), :], gains_ref[shard]],
            axis=1,
        )

    def from_core(slot):
        copy(part.at[me], core_in.at[slot], core_send.at[slot], core_recv.at[slot], partner).wait_recv()
        return core_in[slot].astype(F32)

    def from_side(slot):
        copy(part.at[me], side_in.at[slot], side_send.at[slot], side_recv.at[slot], beside).wait_recv()
        return side_in[slot].astype(F32)

    targets = [lax.rem(line + s, lines) for s in range(1, lines)] + [line]
    for which in (1 - side, side):
        for target in targets:
            shard = spot(target, which, 1 - core)
            slot = target * 2 + which
            part[shard] = load(shard)
            send(part.at[shard], core_in.at[slot], core_send.at[slot], core_recv.at[slot], partner)
    for target in targets:
        shard = spot(target, 1 - side, core)
        part[shard] = (load(shard).astype(F32) + from_core(target * 2 + 1 - side)).astype(BF16)
        send(part.at[shard], side_in.at[target], side_send.at[target], side_recv.at[target], beside)
    for s, target in enumerate(targets):
        shard = spot(target, side, core)
        total = load(shard).astype(F32) + from_core(target * 2 + side) + from_side(target)
        if s < lines - 1:
            part[shard] = total.astype(BF16)
            send(part.at[shard], line_in.at[s], line_send.at[s], line_recv.at[s], across[s])
    for s in range(lines - 1):
        copy(part.at[me], line_in.at[s], line_send.at[s], line_recv.at[s], across[s]).wait_recv()
        total = total + line_in[s].astype(F32)
    mine[...] = total.astype(BF16)
    for s, peer in enumerate(others):
        send(mine, sp_in.at[s], sp_send.at[s], sp_recv.at[s], peer)
    total = mine[...].astype(F32)
    for s, peer in enumerate(others):
        copy(mine, sp_in.at[s], sp_send.at[s], sp_recv.at[s], peer).wait_recv()
        total = total + sp_in[s].astype(F32)
    o_ref[...] = total
    for made in started:
        made.wait_send()


def scatter_packed(grad_fac, grad_out, grad_gains, count, shards):
    rows = grad_fac.shape[0] // count
    columns = grad_fac.shape[1] + grad_out.shape[1] + grad_gains.shape[2]
    lines = count // 4
    buffer = lambda n: pltpu.VMEM((n, rows, columns), BF16)
    sems = lambda n: pltpu.SemaphoreType.DMA((n,))
    return pl.pallas_call(
        functools.partial(scatter_kernel, count=count, shards=shards),
        out_shape=jax.ShapeDtypeStruct((rows, columns), F32),
        in_specs=[pl.BlockSpec(memory_space=pltpu.VMEM)] * 3,
        out_specs=pl.BlockSpec(memory_space=pltpu.VMEM),
        scratch_shapes=[
            buffer(count), buffer(2 * lines), buffer(lines), buffer(lines - 1),
            pltpu.VMEM((rows, columns), BF16), buffer(shards - 1),
            sems(2 * lines), sems(2 * lines), sems(lines), sems(lines),
            sems(lines - 1), sems(lines - 1), sems(shards - 1), sems(shards - 1),
        ],
        compiler_params=pltpu.CompilerParams(collective_id=1, has_side_effects=True),
        name="scatter_packed",
    )(grad_fac, grad_out, grad_gains)


def gather_shards(values, shards):
    me = lax.axis_index("sp")
    rows = values.shape[0]
    full = jnp.zeros((rows * shards,) + values.shape[1:], values.dtype)
    zeros = (0,) * (values.ndim - 1)
    full = lax.dynamic_update_slice(full, values, (me * rows,) + zeros)
    for shift in range(1, shards):
        part = lax.ppermute(values, "sp", [(i, (i + shift) % shards) for i in range(shards)])
        full = lax.dynamic_update_slice(full, part, (((me - shift) % shards) * rows,) + zeros)
    return full


def sum_shards(values, shards):
    if shards == 2:
        other = lax.ppermute(values, "sp", [(0, 1), (1, 0)])
        return values.astype(F32) + other.astype(F32)
    return lax.psum(values, "sp").astype(F32)


def arrange_factor(w, shards):
    heads = H // shards
    spans = ((0, RQ), (H * RQ, RK), (H * (RQ + RK), RK))
    parts = [w[:, H * RANKS :]]
    for device in range(shards):
        own = [
            w[:, base + device * heads * r : base + (device + 1) * heads * r] for base, r in spans
        ]
        parts.append(jnp.pad(jnp.concatenate(own, axis=1), ((0, 0), (0, LANES - heads * RANKS))))
    return jnp.concatenate(parts, axis=1)


def restore_factor(g, shards):
    heads = H // shards
    spans = ((0, RQ), (heads * RQ, RK), (heads * (RQ + RK), RK))
    parts = []
    for base, r in spans:
        for device in range(shards):
            begin = NB + device * LANES + base
            parts.append(g[:, begin : begin + heads * r])
    parts.append(g[:, :NB])
    return jnp.concatenate(parts, axis=1)


def local(tokens, segments, cotangent, gain_attn, w_fac, w_out, gain_ffn, w_gu, w_down, shards, count):
    me = lax.axis_index("sp")
    features = tokens.shape[2]
    heads = H // shards
    columns = heads * DH
    fac_columns = NB + shards * LANES
    own_rows = w_fac.shape[0]

    gains = jnp.concatenate([gain_attn, gain_ffn])[None]
    gains = jnp.pad(gains, ((0, own_rows - 1), (0, LANES - 2 * own_rows)))
    packed = jnp.concatenate([arrange_factor(w_fac, shards), w_out, gains], axis=1)
    packed = gather_packed(packed, count)
    gu_full = lax.all_gather(w_gu, "fsdp", axis=0, tiled=True)
    down_full = lax.all_gather(w_down, "fsdp", axis=0, tiled=True)
    gains = packed[:, 0, fac_columns + features :].astype(F32)
    gain_one = gains[:, :own_rows].reshape(1, features)
    gain_two = gains[:, own_rows : 2 * own_rows].reshape(1, features)
    packed = packed.reshape(features, packed.shape[2])
    fac_full = packed[:, :fac_columns]
    out_full = packed[:, fac_columns : fac_columns + features]

    tokens_all = gather_shards(tokens[0], shards)
    seg_all = gather_shards(segments[0], shards)
    own_left = lax.dynamic_slice_in_dim(fac_full, NB + me * LANES, LANES, 1)
    own_weights = jnp.concatenate([fac_full[:, :NB], own_left], axis=1)
    spreader = expansion(heads)
    factors, query_heads, key_heads, value_heads = heads_forward(
        tokens_all, gain_one, own_weights, spreader, columns
    )
    mixed_heads = attend_forward(query_heads, key_heads, value_heads, seg_all)
    mixed_tokens = lax.all_to_all(mixed_heads, "sp", split_axis=0, concat_axis=1, tiled=True)

    inputs = tokens[0].astype(F32)
    token_count = inputs.shape[0]
    hidden_in = inputs + product(mixed_tokens, out_full)
    normed_two = rms_norm(hidden_in, gain_two).astype(BF16)
    gate_up = product(normed_two, gu_full)
    activated = swiglu(gate_up).astype(BF16)
    grad_out = cotangent[0].astype(F32)
    grad_low = cotangent[0]
    grad_down = weight_grad(activated, grad_low).astype(BF16)
    grad_down = lax.psum_scatter(grad_down, "fsdp", scatter_dimension=0, tiled=True)

    result = hidden_in + product(activated, down_full)
    output = result.astype(BF16)[None]

    grad_act = back_product(grad_low, down_full)
    _, pull_ffn = jax.vjp(swiglu, gate_up)
    grad_gate_up = pull_ffn(grad_act)[0].astype(BF16)
    grad_gu = weight_grad(normed_two, grad_gate_up).astype(BF16)
    grad_gu = lax.psum_scatter(grad_gu, "fsdp", scatter_dimension=0, tiled=True)
    grad_normed_two = back_product(grad_gate_up, gu_full)
    _, pull_two = jax.vjp(rms_norm, hidden_in, gain_two)
    grad_from_norm, grad_gain_two = pull_two(grad_normed_two)
    grad_hidden = grad_out + grad_from_norm
    grad_branch = grad_hidden.astype(BF16)
    grad_wout = weight_grad(mixed_tokens, grad_branch)
    grad_mixed = back_product(grad_branch, out_full).astype(BF16)
    grad_heads = lax.all_to_all(grad_mixed, "sp", split_axis=1, concat_axis=0, tiled=True)
    grad_q, grad_k, grad_v = attend_backward(
        query_heads, key_heads, value_heads, grad_heads, seg_all
    )
    grad_parts = heads_backward(factors, spreader, grad_q, grad_k, grad_v)
    grad_parts = lax.all_to_all(
        grad_parts.reshape(shards, token_count, NB + LANES), "sp", split_axis=0, concat_axis=0
    )
    grad_right = jnp.sum(grad_parts[:, :, :NB].astype(F32), axis=0).astype(BF16)
    grad_factor = jnp.concatenate(
        [grad_right] + [grad_parts[device, :, NB:] for device in range(shards)], axis=1
    )
    normed_one = rms_norm(inputs, gain_one).astype(BF16)
    grad_fac = weight_grad(normed_one, grad_factor)
    grad_normed_one = back_product(grad_factor, fac_full)
    _, pull_one = jax.vjp(rms_norm, inputs, gain_one)
    grad_in_norm, grad_gain_one = pull_one(grad_normed_one)
    grad_tokens = (grad_hidden + grad_in_norm).reshape(1, token_count, features)

    grad_gains = jnp.concatenate(
        [grad_gain_one.reshape(count, own_rows), grad_gain_two.reshape(count, own_rows)], axis=1
    )
    grad_gains = jnp.pad(
        grad_gains[:, None], ((0, 0), (0, own_rows - 1), (0, LANES - 2 * own_rows))
    )
    grad_packed = scatter_packed(
        grad_fac.astype(BF16), grad_wout.astype(BF16), grad_gains.astype(BF16), count, shards
    )
    grad_down = sum_shards(grad_down, shards)
    grad_gu = sum_shards(grad_gu, shards)
    gain_row = grad_packed[0, fac_columns + features :]
    return (
        output,
        grad_tokens,
        gain_row[:own_rows],
        restore_factor(grad_packed[:, :fac_columns], shards),
        grad_packed[:, fac_columns : fac_columns + features],
        gain_row[own_rows : 2 * own_rows],
        grad_gu,
        grad_down,
    )


def solution(mesh):
    in_specs = (
        P("fsdp", "sp", None),
        P("fsdp", "sp"),
        P("fsdp", "sp", None),
        P("fsdp"),
        P("fsdp", None),
        P("fsdp", None),
        P("fsdp"),
        P("fsdp", None),
        P("fsdp", None),
    )
    out_specs = (
        P("fsdp", "sp", None),
        P("fsdp", "sp", None),
        P("fsdp"),
        P("fsdp", None),
        P("fsdp", None),
        P("fsdp"),
        P("fsdp", None),
        P("fsdp", None),
    )

    def body(*args):
        return local(*args, shards=mesh.shape["sp"], count=mesh.shape["fsdp"])

    return jax.shard_map(body, mesh=mesh, in_specs=in_specs, out_specs=out_specs, check_vma=False)
```

```python
import functools

import jax
import jax.numpy as jnp
from jax import lax
from jax.experimental import pallas as pl
from jax.experimental.pallas import tpu as pltpu
from jax.sharding import PartitionSpec as P


H = 16
DH = 64
RQ = 6
RK = 2
FF = 2816
LANES = 128
NB = (RQ + 2 * RK) * DH
RANKS = RQ + 2 * RK
MOVED = 768

EPSILON = 1e-06
NEG = -1e30
F32 = jnp.float32
BF16 = jnp.bfloat16


def rms_norm(values, gain_row):
    factor = lax.rsqrt(jnp.mean(values * values, axis=-1, keepdims=True) + EPSILON)
    return values * factor * gain_row


def swiglu(gate_up):
    return jax.nn.silu(gate_up[:, :FF]) * gate_up[:, FF:]


def product(left, right):
    return jnp.dot(left, right, preferred_element_type=F32)


def weight_grad(left, right):
    return jnp.einsum("ta,tb->ab", left, right, preferred_element_type=F32)


def back_product(grad_rows, weight):
    return jnp.einsum("tb,ab->ta", grad_rows, weight, preferred_element_type=F32)


def dot_nt(a, b):
    return lax.dot_general(a, b, (((1,), (1,)), ((), ())), preferred_element_type=F32)


def dot_tn(a, b):
    return lax.dot_general(a, b, (((0,), (0,)), ((), ())), preferred_element_type=F32)


def band_start(index, block, width):
    return pl.multiple_of(jnp.maximum(index * block - (width - block), 0), LANES)


def band_bias(index, start, seg_col, seg_row, block, width):
    rows = index * block + lax.broadcasted_iota(jnp.int32, (block, width), 0)
    cols = start + lax.broadcasted_iota(jnp.int32, (block, width), 1)
    keep = (seg_col == seg_row) & (cols <= rows)
    return jnp.where(keep, 0.0, NEG)


def half_masks(scale):
    lane = lax.broadcasted_iota(jnp.int32, (1, LANES), 1)
    low = jnp.where(lane < DH, scale, 0.0).astype(BF16)
    high = jnp.where(lane < DH, 0.0, scale).astype(BF16)
    return low, high


def split_pair(values, masks):
    return jnp.concatenate([values * masks[0], values * masks[1]], axis=0)


def attend_forward_kernel(q_ref, k_ref, v_ref, segc_ref, segr_ref, o_ref, *, block, width):
    index = pl.program_id(0)
    start = band_start(index, block, width)
    bias = band_bias(index, start, segc_ref[...], segr_ref[:, pl.ds(start, width)], block, width)
    bias = jnp.concatenate([bias, bias], axis=0)
    masks = half_masks(DH ** (-0.5))
    first = lax.broadcasted_iota(jnp.int32, (block, LANES), 1) < DH
    for pair in range(q_ref.shape[1] // LANES):
        lanes = slice(pair * LANES, (pair + 1) * LANES)
        queries = split_pair(q_ref[:, lanes], masks)
        keys = k_ref[pl.ds(start, width), lanes]
        values = v_ref[pl.ds(start, width), lanes]
        scores = dot_nt(queries, keys) + bias
        exponent = jnp.exp(scores - jnp.max(scores, axis=-1, keepdims=True))
        inverse = 1.0 / jnp.sum(exponent, axis=-1, keepdims=True)
        probs = (exponent * inverse).astype(BF16)
        mixed = product(probs, values)
        o_ref[:, lanes] = jnp.where(first, mixed[:block], mixed[block:]).astype(BF16)


def attend_backward_kernel(
    q_ref, k_ref, v_ref, g_ref, segc_ref, segr_ref, dq_ref, dk_ref, dv_ref, dk_acc, dv_acc,
    *, block, width
):
    index = pl.program_id(0)
    start = band_start(index, block, width)
    scaling = DH ** (-0.5)

    @pl.when(index == 0)
    def _():
        dk_acc[...] = jnp.zeros_like(dk_acc)
        dv_acc[...] = jnp.zeros_like(dv_acc)

    bias = band_bias(index, start, segc_ref[...], segr_ref[:, pl.ds(start, width)], block, width)
    bias = jnp.concatenate([bias, bias], axis=0)
    scale_masks = half_masks(scaling)
    unit_masks = half_masks(1.0)
    first = lax.broadcasted_iota(jnp.int32, (block, LANES), 1) < DH
    window = pl.ds(start, width)
    for pair in range(q_ref.shape[1] // LANES):
        lanes = slice(pair * LANES, (pair + 1) * LANES)
        queries = split_pair(q_ref[:, lanes], scale_masks)
        grads = split_pair(g_ref[:, lanes], unit_masks)
        keys = k_ref[window, lanes]
        values = v_ref[window, lanes]
        scores = dot_nt(queries, keys) + bias
        exponent = jnp.exp(scores - jnp.max(scores, axis=-1, keepdims=True))
        inverse = 1.0 / jnp.sum(exponent, axis=-1, keepdims=True)
        probs = exponent * inverse
        grad_probs = dot_nt(grads, values)
        inner = jnp.sum(probs * grad_probs, axis=-1, keepdims=True)
        grad_scores = (probs * (grad_probs - inner)).astype(BF16)
        grad_q = product(grad_scores, keys) * scaling
        dq_ref[:, lanes] = jnp.where(first, grad_q[:block], grad_q[block:]).astype(BF16)
        dk_acc[window, lanes] += dot_tn(grad_scores, queries)
        dv_acc[window, lanes] += dot_tn(probs.astype(BF16), grads)

    @pl.when(index == pl.num_programs(0) - 1)
    def _():
        dk_ref[...] = dk_acc[...].astype(BF16)
        dv_ref[...] = dv_acc[...].astype(BF16)


def attention_specs(length, columns):
    block = LANES
    width = min(length // 4 + block, length)
    whole = pl.BlockSpec((length, columns), lambda i: (0, 0))
    rows = pl.BlockSpec((block, columns), lambda i: (i, 0))
    seg_col = pl.BlockSpec((block, 1), lambda i: (i, 0))
    seg_row = pl.BlockSpec((1, length), lambda i: (0, 0))
    return block, width, whole, rows, seg_col, seg_row


def attend_forward(queries, keys, values, seg_all):
    length, columns = queries.shape
    block, width, whole, rows, seg_col, seg_row = attention_specs(length, columns)
    work = length * width * columns
    return pl.pallas_call(
        functools.partial(attend_forward_kernel, block=block, width=width),
        grid=(length // block,),
        in_specs=[rows, whole, whole, seg_col, seg_row],
        out_specs=rows,
        out_shape=jax.ShapeDtypeStruct((length, columns), BF16),
        cost_estimate=pl.CostEstimate(
            flops=16 * work, bytes_accessed=8 * length * columns, transcendentals=work // DH
        ),
        name="attend_forward",
    )(queries, keys, values, seg_all.reshape(length, 1), seg_all.reshape(1, length))


def attend_backward(queries, keys, values, grads, seg_all):
    length, columns = queries.shape
    block, width, whole, rows, seg_col, seg_row = attention_specs(length, columns)
    work = length * width * columns
    shape = jax.ShapeDtypeStruct((length, columns), BF16)
    return pl.pallas_call(
        functools.partial(attend_backward_kernel, block=block, width=width),
        grid=(length // block,),
        in_specs=[rows, whole, whole, rows, seg_col, seg_row],
        out_specs=[rows, whole, whole],
        out_shape=[shape, shape, shape],
        scratch_shapes=[pltpu.VMEM((length, columns), F32), pltpu.VMEM((length, columns), F32)],
        cost_estimate=pl.CostEstimate(
            flops=40 * work, bytes_accessed=14 * length * columns, transcendentals=work // DH
        ),
        name="attend_backward",
    )(queries, keys, values, grads, seg_all.reshape(length, 1), seg_all.reshape(1, length))


def expansion(heads):
    rows = lax.broadcasted_iota(jnp.int32, (2 * LANES, RANKS * heads * DH), 0) % LANES
    cols = lax.broadcasted_iota(jnp.int32, (2 * LANES, RANKS * heads * DH), 1)
    rank, head = cols // (heads * DH), (cols % (heads * DH)) // DH
    in_k = heads * RQ + head * RK + rank - RQ
    in_v = heads * (RQ + RK) + head * RK + rank - RQ - RK
    source = jnp.where(
        rank < RQ, head * RQ + rank, jnp.where(rank < RQ + RK, in_k, in_v)
    )
    return (rows == source).astype(BF16)


def high_low(values):
    high = values.astype(BF16)
    return high, (values - high.astype(F32)).astype(BF16)


def doubled(factor, rank, first):
    pair = factor[:, (rank // 2) * LANES : (rank // 2 + 1) * LANES]
    turned = pltpu.roll(pair, DH, 1)
    return jnp.where(first, pair, turned) if rank % 2 == 0 else jnp.where(first, turned, pair)


GROUPS = ((0, RQ), (RQ, RK), (RQ + RK, RK))


def heads_forward_kernel(x_ref, gain_ref, w_ref, e_ref, f_ref, q_ref, k_ref, v_ref):
    normed = rms_norm(x_ref[...].astype(F32), gain_ref[...]).astype(BF16)
    factor = product(normed, w_ref[...])
    f_ref[...] = factor
    spread = jnp.concatenate(high_low(factor[:, NB:]), axis=1)
    rows, columns = q_ref.shape
    first = lax.broadcasted_iota(jnp.int32, (rows, LANES), 1) < DH
    for (base, ranks), out_ref in zip(GROUPS, (q_ref, k_ref, v_ref)):
        total = None
        for rank in range(base, base + ranks):
            left = product(spread, e_ref[:, rank * columns : (rank + 1) * columns])
            right = jnp.concatenate([doubled(factor, rank, first)] * (columns // LANES), axis=1)
            total = left * right if total is None else total + left * right
        out_ref[...] = (total * (1.0 / ranks)).astype(BF16)


def heads_backward_kernel(f_ref, e_ref, dq_ref, dk_ref, dv_ref, g_ref):
    factor = f_ref[...]
    spread = jnp.concatenate(high_low(factor[:, NB:]), axis=1)
    rows, columns = dq_ref.shape
    first = lax.broadcasted_iota(jnp.int32, (rows, LANES), 1) < DH
    left_total = jnp.zeros((rows, LANES), F32)
    folded = []
    for (base, ranks), grad_ref in zip(GROUPS, (dq_ref, dk_ref, dv_ref)):
        grad = grad_ref[...].astype(F32) * (1.0 / ranks)
        for rank in range(base, base + ranks):
            ones = e_ref[:, rank * columns : (rank + 1) * columns]
            weighted = product(spread, ones) * grad
            right_grad = weighted[:, :LANES]
            for chunk in range(1, columns // LANES):
                right_grad = right_grad + weighted[:, chunk * LANES : (chunk + 1) * LANES]
            folded.append(right_grad + pltpu.roll(right_grad, DH, 1))
            right = jnp.concatenate([doubled(factor, rank, first)] * (columns // LANES), axis=1)
            high, low = high_low(grad * right)
            left_total = left_total + dot_nt(high, ones[:LANES]) + dot_nt(low, ones[:LANES])
    for pair in range(RANKS // 2):
        g_ref[:, pair * LANES : (pair + 1) * LANES] = jnp.where(
            first, folded[2 * pair], folded[2 * pair + 1]
        ).astype(BF16)
    g_ref[:, NB:] = left_total.astype(BF16)


HEAD_ROWS = 256


def heads_forward(tokens, gain_row, weights, spreader, columns):
    length, width = tokens.shape
    rows = min(HEAD_ROWS, length)
    block = lambda n: pl.BlockSpec((rows, n), lambda i: (i, 0))
    fixed = lambda a: pl.BlockSpec(a.shape, lambda i: (0, 0))
    head = jax.ShapeDtypeStruct((length, columns), BF16)
    return pl.pallas_call(
        heads_forward_kernel,
        grid=(length // rows,),
        in_specs=[block(width), fixed(gain_row), fixed(weights), fixed(spreader)],
        out_specs=[block(NB + LANES)] + [block(columns)] * 3,
        out_shape=[jax.ShapeDtypeStruct((length, NB + LANES), F32), head, head, head],
        name="heads_forward",
    )(tokens, gain_row, weights, spreader)


def heads_backward(factors, spreader, grad_q, grad_k, grad_v):
    length, columns = grad_q.shape
    rows = min(HEAD_ROWS, length)
    block = lambda n: pl.BlockSpec((rows, n), lambda i: (i, 0))
    return pl.pallas_call(
        heads_backward_kernel,
        grid=(length // rows,),
        in_specs=[
            block(NB + LANES), pl.BlockSpec(spreader.shape, lambda i: (0, 0)),
            block(columns), block(columns), block(columns),
        ],
        out_specs=block(NB + LANES),
        out_shape=jax.ShapeDtypeStruct((length, NB + LANES), BF16),
        name="heads_backward",
    )(factors, spreader, grad_q, grad_k, grad_v)


MESH_ID = pl.DeviceIdType.MESH


def place(count):
    me = lax.axis_index("fsdp")
    line, side, core = me // 4, (me // 2) % 2, me % 2
    return me, line, side, core, count // 4


def spot(line, side, core):
    return (line * 2 + side) * 2 + core


def meet(peers):
    barrier = pltpu.get_barrier_semaphore()
    for peer in peers:
        pl.semaphore_signal(barrier, inc=1, device_id=peer, device_id_type=MESH_ID)
    pl.semaphore_wait(barrier, len(peers))


def gather_kernel(x_ref, o_ref, local_sem, send_sem, recv_sem, *, count):
    me, line, side, core, lines = place(count)
    across = [{"fsdp": spot(lax.rem(line + s, lines), side, core)} for s in range(1, lines)]
    beside, partner = {"fsdp": spot(line, 1 - side, core)}, {"fsdp": spot(line, side, 1 - core)}
    meet(across + [beside, partner])
    sends = []

    def copy(src, shard, slot, peer):
        return pltpu.make_async_remote_copy(
            src_ref=src, dst_ref=o_ref.at[shard], send_sem=send_sem.at[slot],
            recv_sem=recv_sem.at[shard], device_id=peer, device_id_type=MESH_ID,
        )

    def send(src, shard, peer):
        made = copy(src, shard, len(sends), peer)
        made.start()
        sends.append(made)

    def arrive(shard):
        copy(o_ref.at[shard], shard, 0, partner).wait_recv()

    own = pltpu.make_async_copy(x_ref, o_ref.at[me], local_sem)
    own.start()
    for peer in across:
        send(x_ref, me, peer)
    send(x_ref, me, beside)
    send(x_ref, me, partner)
    sources = [lax.rem(line + lines - s, lines) for s in range(1, lines)]
    for source in sources:
        shard = spot(source, side, core)
        arrive(shard)
        send(o_ref.at[shard], shard, beside)
        send(o_ref.at[shard], shard, partner)
    for source in [line] + sources:
        shard = spot(source, 1 - side, core)
        arrive(shard)
        send(o_ref.at[shard], shard, partner)
    for source in [line] + sources:
        arrive(spot(source, side, 1 - core))
        arrive(spot(source, 1 - side, 1 - core))
    own.wait()
    for made in sends:
        made.wait_send()


def gather_packed(values, count):
    lines = count // 4
    full = pl.pallas_call(
        functools.partial(gather_kernel, count=count),
        out_shape=jax.ShapeDtypeStruct((count,) + values.shape, values.dtype),
        in_specs=[pl.BlockSpec(memory_space=pltpu.VMEM)],
        out_specs=pl.BlockSpec(memory_space=pltpu.VMEM),
        scratch_shapes=[
            pltpu.SemaphoreType.DMA,
            pltpu.SemaphoreType.DMA((4 * lines - 1,)),
            pltpu.SemaphoreType.DMA((count,)),
        ],
        compiler_params=pltpu.CompilerParams(collective_id=0, has_side_effects=True),
        name="gather_packed",
    )(values)
    return full


def scatter_kernel(
    fac_ref, out_ref, rest_ref, gains_ref, o_ref, part, core_in, side_in, line_in, mine, sp_in,
    core_send, core_recv, side_send, side_recv, line_send, line_recv, sp_send, sp_recv,
    *, count, shards
):
    me, line, side, core, lines = place(count)
    rank = lax.axis_index("sp")
    rows = o_ref.shape[0]
    across = [{"fsdp": spot(lax.rem(line + s, lines), side, core)} for s in range(1, lines)]
    beside, partner = {"fsdp": spot(line, 1 - side, core)}, {"fsdp": spot(line, side, 1 - core)}
    others = [{"sp": lax.rem(rank + s, shards)} for s in range(1, shards)]
    meet(across + [beside, partner] + others)
    started = []

    def copy(src, dst, send_sem, recv_sem, peer):
        return pltpu.make_async_remote_copy(
            src_ref=src, dst_ref=dst, send_sem=send_sem, recv_sem=recv_sem,
            device_id=peer, device_id_type=MESH_ID,
        )

    def send(*args):
        made = copy(*args)
        made.start()
        started.append(made)

    def load(shard):
        begin = pl.multiple_of(shard * rows, rows)
        return jnp.concatenate(
            [ref[pl.ds(begin, rows), :] for ref in (fac_ref, out_ref, rest_ref)]
            + [gains_ref[shard]],
            axis=1,
        )

    def from_core(slot):
        copy(part.at[me], core_in.at[slot], core_send.at[slot], core_recv.at[slot], partner).wait_recv()
        return core_in[slot].astype(F32)

    def from_side(slot):
        copy(part.at[me], side_in.at[slot], side_send.at[slot], side_recv.at[slot], beside).wait_recv()
        return side_in[slot].astype(F32)

    targets = [lax.rem(line + s, lines) for s in range(1, lines)] + [line]
    for which in (1 - side, side):
        for target in targets:
            shard = spot(target, which, 1 - core)
            slot = target * 2 + which
            part[shard] = load(shard)
            send(part.at[shard], core_in.at[slot], core_send.at[slot], core_recv.at[slot], partner)
    for target in targets:
        shard = spot(target, 1 - side, core)
        part[shard] = (load(shard).astype(F32) + from_core(target * 2 + 1 - side)).astype(BF16)
        send(part.at[shard], side_in.at[target], side_send.at[target], side_recv.at[target], beside)
    for s, target in enumerate(targets):
        shard = spot(target, side, core)
        total = load(shard).astype(F32) + from_core(target * 2 + side) + from_side(target)
        if s < lines - 1:
            part[shard] = total.astype(BF16)
            send(part.at[shard], line_in.at[s], line_send.at[s], line_recv.at[s], across[s])
    for s in range(lines - 1):
        copy(part.at[me], line_in.at[s], line_send.at[s], line_recv.at[s], across[s]).wait_recv()
        total = total + line_in[s].astype(F32)
    mine[...] = total.astype(BF16)
    for s, peer in enumerate(others):
        send(mine, sp_in.at[s], sp_send.at[s], sp_recv.at[s], peer)
    total = mine[...].astype(F32)
    for s, peer in enumerate(others):
        copy(mine, sp_in.at[s], sp_send.at[s], sp_recv.at[s], peer).wait_recv()
        total = total + sp_in[s].astype(F32)
    o_ref[...] = total
    for made in started:
        made.wait_send()


def scatter_packed(grad_fac, grad_out, grad_rest, grad_gains, count, shards):
    rows = grad_fac.shape[0] // count
    columns = sum(a.shape[-1] for a in (grad_fac, grad_out, grad_rest, grad_gains))
    lines = count // 4
    buffer = lambda n: pltpu.VMEM((n, rows, columns), BF16)
    sems = lambda n: pltpu.SemaphoreType.DMA((n,))
    return pl.pallas_call(
        functools.partial(scatter_kernel, count=count, shards=shards),
        out_shape=jax.ShapeDtypeStruct((rows, columns), F32),
        in_specs=[pl.BlockSpec(memory_space=pltpu.VMEM)] * 4,
        out_specs=pl.BlockSpec(memory_space=pltpu.VMEM),
        scratch_shapes=[
            buffer(count), buffer(2 * lines), buffer(lines), buffer(lines - 1),
            pltpu.VMEM((rows, columns), BF16), buffer(shards - 1),
            sems(2 * lines), sems(2 * lines), sems(lines), sems(lines),
            sems(lines - 1), sems(lines - 1), sems(shards - 1), sems(shards - 1),
        ],
        compiler_params=pltpu.CompilerParams(collective_id=1, has_side_effects=True),
        name="scatter_packed",
    )(grad_fac, grad_out, grad_rest, grad_gains)


def gather_shards(values, shards):
    me = lax.axis_index("sp")
    rows = values.shape[0]
    full = jnp.zeros((rows * shards,) + values.shape[1:], values.dtype)
    zeros = (0,) * (values.ndim - 1)
    full = lax.dynamic_update_slice(full, values, (me * rows,) + zeros)
    for shift in range(1, shards):
        part = lax.ppermute(values, "sp", [(i, (i + shift) % shards) for i in range(shards)])
        full = lax.dynamic_update_slice(full, part, (((me - shift) % shards) * rows,) + zeros)
    return full


def sum_shards(values, shards):
    if shards == 2:
        other = lax.ppermute(values, "sp", [(0, 1), (1, 0)])
        return values.astype(F32) + other.astype(F32)
    return lax.psum(values, "sp").astype(F32)


def arrange_factor(w, shards):
    heads = H // shards
    spans = ((0, RQ), (H * RQ, RK), (H * (RQ + RK), RK))
    parts = [w[:, H * RANKS :]]
    for device in range(shards):
        own = [
            w[:, base + device * heads * r : base + (device + 1) * heads * r] for base, r in spans
        ]
        parts.append(jnp.pad(jnp.concatenate(own, axis=1), ((0, 0), (0, LANES - heads * RANKS))))
    return jnp.concatenate(parts, axis=1)


def restore_factor(g, shards):
    heads = H // shards
    spans = ((0, RQ), (heads * RQ, RK), (heads * (RQ + RK), RK))
    parts = []
    for base, r in spans:
        for device in range(shards):
            begin = NB + device * LANES + base
            parts.append(g[:, begin : begin + heads * r])
    parts.append(g[:, :NB])
    return jnp.concatenate(parts, axis=1)


def local(tokens, segments, cotangent, gain_attn, w_fac, w_out, gain_ffn, w_gu, w_down, shards, count):
    me = lax.axis_index("sp")
    features = tokens.shape[2]
    heads = H // shards
    columns = heads * DH
    fac_columns = NB + shards * LANES
    own_rows = w_fac.shape[0]

    gains = jnp.concatenate([gain_attn, gain_ffn])[None]
    gains = jnp.pad(gains, ((0, own_rows - 1), (0, LANES - 2 * own_rows)))
    packed = jnp.concatenate([arrange_factor(w_fac, shards), w_out, gains], axis=1)
    packed = gather_packed(packed, count)
    gu_full = lax.all_gather(w_gu, "fsdp", axis=0, tiled=True)
    down_full = lax.all_gather(w_down, "fsdp", axis=0, tiled=True)
    gains = packed[:, 0, fac_columns + features :].astype(F32)
    gain_one = gains[:, :own_rows].reshape(1, features)
    gain_two = gains[:, own_rows : 2 * own_rows].reshape(1, features)
    packed = packed.reshape(features, packed.shape[2])
    fac_full = packed[:, :fac_columns]
    out_full = packed[:, fac_columns : fac_columns + features]

    tokens_all = gather_shards(tokens[0], shards)
    seg_all = gather_shards(segments[0], shards)
    own_left = lax.dynamic_slice_in_dim(fac_full, NB + me * LANES, LANES, 1)
    own_weights = jnp.concatenate([fac_full[:, :NB], own_left], axis=1)
    spreader = expansion(heads)
    factors, query_heads, key_heads, value_heads = heads_forward(
        tokens_all, gain_one, own_weights, spreader, columns
    )
    mixed_heads = attend_forward(query_heads, key_heads, value_heads, seg_all)
    mixed_tokens = lax.all_to_all(mixed_heads, "sp", split_axis=0, concat_axis=1, tiled=True)

    inputs = tokens[0].astype(F32)
    token_count = inputs.shape[0]
    hidden_in = inputs + product(mixed_tokens, out_full)
    normed_two = rms_norm(hidden_in, gain_two).astype(BF16)
    gate_up = product(normed_two, gu_full)
    activated = swiglu(gate_up).astype(BF16)
    gate_up, activated = lax.optimization_barrier((gate_up, activated))
    grad_out = cotangent[0].astype(F32)
    grad_low = cotangent[0]
    grad_down = weight_grad(activated, grad_low).astype(BF16)
    grad_down = lax.psum_scatter(grad_down, "fsdp", scatter_dimension=0, tiled=True)

    result = hidden_in + product(activated, down_full)
    output = result.astype(BF16)[None]

    grad_act = back_product(grad_low, down_full)
    _, pull_ffn = jax.vjp(swiglu, gate_up)
    grad_gate_up = pull_ffn(grad_act)[0].astype(BF16)
    kept = grad_gate_up.shape[1] - MOVED
    grad_rest = weight_grad(normed_two, grad_gate_up[:, kept:]).astype(BF16)
    grad_gu = weight_grad(normed_two, grad_gate_up[:, :kept]).astype(BF16)
    grad_gu = lax.psum_scatter(grad_gu, "fsdp", scatter_dimension=0, tiled=True)
    grad_normed_two = back_product(grad_gate_up, gu_full)
    _, pull_two = jax.vjp(rms_norm, hidden_in, gain_two)
    grad_from_norm, grad_gain_two = pull_two(grad_normed_two)
    grad_hidden = grad_out + grad_from_norm
    grad_branch = grad_hidden.astype(BF16)
    grad_wout = weight_grad(mixed_tokens, grad_branch)
    grad_mixed = back_product(grad_branch, out_full).astype(BF16)
    grad_heads = lax.all_to_all(grad_mixed, "sp", split_axis=1, concat_axis=0, tiled=True)
    grad_q, grad_k, grad_v = attend_backward(
        query_heads, key_heads, value_heads, grad_heads, seg_all
    )
    grad_parts = heads_backward(factors, spreader, grad_q, grad_k, grad_v)
    grad_parts = lax.all_to_all(
        grad_parts.reshape(shards, token_count, NB + LANES), "sp", split_axis=0, concat_axis=0
    )
    grad_right = jnp.sum(grad_parts[:, :, :NB].astype(F32), axis=0).astype(BF16)
    grad_factor = jnp.concatenate(
        [grad_right] + [grad_parts[device, :, NB:] for device in range(shards)], axis=1
    )
    normed_one = rms_norm(inputs, gain_one).astype(BF16)
    grad_fac = weight_grad(normed_one, grad_factor)
    grad_normed_one = back_product(grad_factor, fac_full)
    _, pull_one = jax.vjp(rms_norm, inputs, gain_one)
    grad_in_norm, grad_gain_one = pull_one(grad_normed_one)
    grad_tokens = (grad_hidden + grad_in_norm).reshape(1, token_count, features)

    grad_gains = jnp.concatenate(
        [grad_gain_one.reshape(count, own_rows), grad_gain_two.reshape(count, own_rows)], axis=1
    )
    grad_gains = jnp.pad(
        grad_gains[:, None], ((0, 0), (0, own_rows - 1), (0, LANES - 2 * own_rows))
    )
    grad_packed = scatter_packed(
        grad_fac.astype(BF16), grad_wout.astype(BF16), grad_rest, grad_gains.astype(BF16),
        count, shards,
    )
    grad_down = sum_shards(grad_down, shards)
    grad_gu = sum_shards(grad_gu, shards)
    tail = fac_columns + features
    gain_row = grad_packed[0, tail + MOVED :]
    grad_gu = jnp.concatenate([grad_gu, grad_packed[:, tail : tail + MOVED]], axis=1)
    return (
        output,
        grad_tokens,
        gain_row[:own_rows],
        restore_factor(grad_packed[:, :fac_columns], shards),
        grad_packed[:, fac_columns : fac_columns + features],
        gain_row[own_rows : 2 * own_rows],
        grad_gu,
        grad_down,
    )


def solution(mesh):
    in_specs = (
        P("fsdp", "sp", None),
        P("fsdp", "sp"),
        P("fsdp", "sp", None),
        P("fsdp"),
        P("fsdp", None),
        P("fsdp", None),
        P("fsdp"),
        P("fsdp", None),
        P("fsdp", None),
    )
    out_specs = (
        P("fsdp", "sp", None),
        P("fsdp", "sp", None),
        P("fsdp"),
        P("fsdp", None),
        P("fsdp", None),
        P("fsdp"),
        P("fsdp", None),
        P("fsdp", None),
    )

    def body(*args):
        return local(*args, shards=mesh.shape["sp"], count=mesh.shape["fsdp"])

    return jax.shard_map(body, mesh=mesh, in_specs=in_specs, out_specs=out_specs, check_vma=False)
```

```python
import functools

import jax
import jax.numpy as jnp
from jax import lax
from jax.experimental import pallas as pl
from jax.experimental.pallas import tpu as pltpu
from jax.sharding import PartitionSpec as P


H = 16
DH = 64
RQ = 6
RK = 2
FF = 2816
LANES = 128
NB = (RQ + 2 * RK) * DH
RANKS = RQ + 2 * RK
MOVED = 1792

EPSILON = 1e-06
NEG = -1e30
F32 = jnp.float32
BF16 = jnp.bfloat16


def rms_norm(values, gain_row):
    factor = lax.rsqrt(jnp.mean(values * values, axis=-1, keepdims=True) + EPSILON)
    return values * factor * gain_row


def swiglu(gate_up):
    return jax.nn.silu(gate_up[:, :FF]) * gate_up[:, FF:]


def product(left, right):
    return jnp.dot(left, right, preferred_element_type=F32)


def weight_grad(left, right):
    return jnp.einsum("ta,tb->ab", left, right, preferred_element_type=F32)


def back_product(grad_rows, weight):
    return jnp.einsum("tb,ab->ta", grad_rows, weight, preferred_element_type=F32)


def dot_nt(a, b):
    return lax.dot_general(a, b, (((1,), (1,)), ((), ())), preferred_element_type=F32)


def dot_tn(a, b):
    return lax.dot_general(a, b, (((0,), (0,)), ((), ())), preferred_element_type=F32)


def band_start(index, block, width):
    return pl.multiple_of(jnp.maximum(index * block - (width - block), 0), LANES)


def band_bias(index, start, seg_col, seg_row, block, width):
    rows = index * block + lax.broadcasted_iota(jnp.int32, (block, width), 0)
    cols = start + lax.broadcasted_iota(jnp.int32, (block, width), 1)
    keep = (seg_col == seg_row) & (cols <= rows)
    return jnp.where(keep, 0.0, NEG)


def half_masks(scale):
    lane = lax.broadcasted_iota(jnp.int32, (1, LANES), 1)
    low = jnp.where(lane < DH, scale, 0.0).astype(BF16)
    high = jnp.where(lane < DH, 0.0, scale).astype(BF16)
    return low, high


def split_pair(values, masks):
    return jnp.concatenate([values * masks[0], values * masks[1]], axis=0)


def attend_forward_kernel(q_ref, k_ref, v_ref, segc_ref, segr_ref, o_ref, *, block, width):
    index = pl.program_id(0)
    start = band_start(index, block, width)
    bias = band_bias(index, start, segc_ref[...], segr_ref[:, pl.ds(start, width)], block, width)
    bias = jnp.concatenate([bias, bias], axis=0)
    masks = half_masks(DH ** (-0.5))
    first = lax.broadcasted_iota(jnp.int32, (block, LANES), 1) < DH

    @pl.loop(0, q_ref.shape[1] // LANES)
    def _(pair):
        lanes = pl.ds(pl.multiple_of(pair * LANES, LANES), LANES)
        queries = split_pair(q_ref[:, lanes], masks)
        keys = k_ref[pl.ds(start, width), lanes]
        values = v_ref[pl.ds(start, width), lanes]
        scores = dot_nt(queries, keys) + bias
        exponent = jnp.exp(scores - jnp.max(scores, axis=-1, keepdims=True))
        inverse = 1.0 / jnp.sum(exponent, axis=-1, keepdims=True)
        probs = (exponent * inverse).astype(BF16)
        mixed = product(probs, values)
        o_ref[:, lanes] = jnp.where(first, mixed[:block], mixed[block:]).astype(BF16)


def attend_backward_kernel(
    q_ref, k_ref, v_ref, g_ref, segc_ref, segr_ref, dq_ref, dk_ref, dv_ref, dk_acc, dv_acc,
    *, block, width
):
    index = pl.program_id(0)
    start = band_start(index, block, width)
    scaling = DH ** (-0.5)

    @pl.when(index == 0)
    def _():
        dk_acc[...] = jnp.zeros_like(dk_acc)
        dv_acc[...] = jnp.zeros_like(dv_acc)

    bias = band_bias(index, start, segc_ref[...], segr_ref[:, pl.ds(start, width)], block, width)
    bias = jnp.concatenate([bias, bias], axis=0)
    scale_masks = half_masks(scaling)
    unit_masks = half_masks(1.0)
    first = lax.broadcasted_iota(jnp.int32, (block, LANES), 1) < DH
    window = pl.ds(start, width)

    @pl.loop(0, q_ref.shape[1] // LANES)
    def _(pair):
        lanes = pl.ds(pl.multiple_of(pair * LANES, LANES), LANES)
        queries = split_pair(q_ref[:, lanes], scale_masks)
        grads = split_pair(g_ref[:, lanes], unit_masks)
        keys = k_ref[window, lanes]
        values = v_ref[window, lanes]
        scores = dot_nt(queries, keys) + bias
        exponent = jnp.exp(scores - jnp.max(scores, axis=-1, keepdims=True))
        inverse = 1.0 / jnp.sum(exponent, axis=-1, keepdims=True)
        probs = exponent * inverse
        grad_probs = dot_nt(grads, values)
        inner = jnp.sum(probs * grad_probs, axis=-1, keepdims=True)
        grad_scores = (probs * (grad_probs - inner)).astype(BF16)
        grad_q = product(grad_scores, keys) * scaling
        dq_ref[:, lanes] = jnp.where(first, grad_q[:block], grad_q[block:]).astype(BF16)
        dk_acc[window, lanes] += dot_tn(grad_scores, queries)
        dv_acc[window, lanes] += dot_tn(probs.astype(BF16), grads)

    @pl.when(index == pl.num_programs(0) - 1)
    def _():
        dk_ref[...] = dk_acc[...].astype(BF16)
        dv_ref[...] = dv_acc[...].astype(BF16)


def attention_specs(length, columns):
    block = LANES
    width = min(length // 4 + block, length)
    whole = pl.BlockSpec((length, columns), lambda i: (0, 0))
    rows = pl.BlockSpec((block, columns), lambda i: (i, 0))
    seg_col = pl.BlockSpec((block, 1), lambda i: (i, 0))
    seg_row = pl.BlockSpec((1, length), lambda i: (0, 0))
    return block, width, whole, rows, seg_col, seg_row


def attend_forward(queries, keys, values, seg_all):
    length, columns = queries.shape
    block, width, whole, rows, seg_col, seg_row = attention_specs(length, columns)
    work = length * width * columns
    return pl.pallas_call(
        functools.partial(attend_forward_kernel, block=block, width=width),
        grid=(length // block,),
        in_specs=[rows, whole, whole, seg_col, seg_row],
        out_specs=rows,
        out_shape=jax.ShapeDtypeStruct((length, columns), BF16),
        cost_estimate=pl.CostEstimate(
            flops=16 * work, bytes_accessed=8 * length * columns, transcendentals=work // DH
        ),
        name="attend_forward",
    )(queries, keys, values, seg_all.reshape(length, 1), seg_all.reshape(1, length))


def attend_backward(queries, keys, values, grads, seg_all):
    length, columns = queries.shape
    block, width, whole, rows, seg_col, seg_row = attention_specs(length, columns)
    work = length * width * columns
    shape = jax.ShapeDtypeStruct((length, columns), BF16)
    return pl.pallas_call(
        functools.partial(attend_backward_kernel, block=block, width=width),
        grid=(length // block,),
        in_specs=[rows, whole, whole, rows, seg_col, seg_row],
        out_specs=[rows, whole, whole],
        out_shape=[shape, shape, shape],
        scratch_shapes=[pltpu.VMEM((length, columns), F32), pltpu.VMEM((length, columns), F32)],
        cost_estimate=pl.CostEstimate(
            flops=40 * work, bytes_accessed=14 * length * columns, transcendentals=work // DH
        ),
        name="attend_backward",
    )(queries, keys, values, grads, seg_all.reshape(length, 1), seg_all.reshape(1, length))


def expansion(heads):
    rows = lax.broadcasted_iota(jnp.int32, (2 * LANES, RANKS * heads * DH), 0) % LANES
    cols = lax.broadcasted_iota(jnp.int32, (2 * LANES, RANKS * heads * DH), 1)
    rank, head = cols // (heads * DH), (cols % (heads * DH)) // DH
    in_k = heads * RQ + head * RK + rank - RQ
    in_v = heads * (RQ + RK) + head * RK + rank - RQ - RK
    source = jnp.where(
        rank < RQ, head * RQ + rank, jnp.where(rank < RQ + RK, in_k, in_v)
    )
    return (rows == source).astype(BF16)


def high_low(values):
    high = values.astype(BF16)
    return high, (values - high.astype(F32)).astype(BF16)


def doubled(factor, rank, first):
    pair = factor[:, (rank // 2) * LANES : (rank // 2 + 1) * LANES]
    turned = pltpu.roll(pair, DH, 1)
    return jnp.where(first, pair, turned) if rank % 2 == 0 else jnp.where(first, turned, pair)


GROUPS = ((0, RQ), (RQ, RK), (RQ + RK, RK))


def heads_forward_kernel(x_ref, gain_ref, w_ref, e_ref, f_ref, q_ref, k_ref, v_ref):
    normed = rms_norm(x_ref[...].astype(F32), gain_ref[...]).astype(BF16)
    factor = product(normed, w_ref[...])
    f_ref[...] = factor
    spread = jnp.concatenate(high_low(factor[:, NB:]), axis=1)
    rows, columns = q_ref.shape
    first = lax.broadcasted_iota(jnp.int32, (rows, LANES), 1) < DH
    for (base, ranks), out_ref in zip(GROUPS, (q_ref, k_ref, v_ref)):
        total = None
        for rank in range(base, base + ranks):
            left = product(spread, e_ref[:, rank * columns : (rank + 1) * columns])
            right = jnp.concatenate([doubled(factor, rank, first)] * (columns // LANES), axis=1)
            total = left * right if total is None else total + left * right
        out_ref[...] = (total * (1.0 / ranks)).astype(BF16)


def heads_backward_kernel(f_ref, e_ref, dq_ref, dk_ref, dv_ref, g_ref):
    factor = f_ref[...]
    spread = jnp.concatenate(high_low(factor[:, NB:]), axis=1)
    rows, columns = dq_ref.shape
    first = lax.broadcasted_iota(jnp.int32, (rows, LANES), 1) < DH
    left_total = jnp.zeros((rows, LANES), F32)
    folded = []
    for (base, ranks), grad_ref in zip(GROUPS, (dq_ref, dk_ref, dv_ref)):
        grad = grad_ref[...].astype(F32) * (1.0 / ranks)
        for rank in range(base, base + ranks):
            ones = e_ref[:, rank * columns : (rank + 1) * columns]
            weighted = product(spread, ones) * grad
            right_grad = weighted[:, :LANES]
            for chunk in range(1, columns // LANES):
                right_grad = right_grad + weighted[:, chunk * LANES : (chunk + 1) * LANES]
            folded.append(right_grad + pltpu.roll(right_grad, DH, 1))
            right = jnp.concatenate([doubled(factor, rank, first)] * (columns // LANES), axis=1)
            high, low = high_low(grad * right)
            left_total = left_total + dot_nt(high, ones[:LANES]) + dot_nt(low, ones[:LANES])
    for pair in range(RANKS // 2):
        g_ref[:, pair * LANES : (pair + 1) * LANES] = jnp.where(
            first, folded[2 * pair], folded[2 * pair + 1]
        ).astype(BF16)
    g_ref[:, NB:] = left_total.astype(BF16)


HEAD_ROWS = 256


def heads_forward(tokens, gain_row, weights, spreader, columns):
    length, width = tokens.shape
    rows = min(HEAD_ROWS, length)
    block = lambda n: pl.BlockSpec((rows, n), lambda i: (i, 0))
    fixed = lambda a: pl.BlockSpec(a.shape, lambda i: (0, 0))
    head = jax.ShapeDtypeStruct((length, columns), BF16)
    return pl.pallas_call(
        heads_forward_kernel,
        grid=(length // rows,),
        in_specs=[block(width), fixed(gain_row), fixed(weights), fixed(spreader)],
        out_specs=[block(NB + LANES)] + [block(columns)] * 3,
        out_shape=[jax.ShapeDtypeStruct((length, NB + LANES), F32), head, head, head],
        name="heads_forward",
    )(tokens, gain_row, weights, spreader)


def heads_backward(factors, spreader, grad_q, grad_k, grad_v):
    length, columns = grad_q.shape
    rows = min(HEAD_ROWS, length)
    block = lambda n: pl.BlockSpec((rows, n), lambda i: (i, 0))
    return pl.pallas_call(
        heads_backward_kernel,
        grid=(length // rows,),
        in_specs=[
            block(NB + LANES), pl.BlockSpec(spreader.shape, lambda i: (0, 0)),
            block(columns), block(columns), block(columns),
        ],
        out_specs=block(NB + LANES),
        out_shape=jax.ShapeDtypeStruct((length, NB + LANES), BF16),
        name="heads_backward",
    )(factors, spreader, grad_q, grad_k, grad_v)


MESH_ID = pl.DeviceIdType.MESH


def place(count):
    me = lax.axis_index("fsdp")
    line, side, core = me // 4, (me // 2) % 2, me % 2
    return me, line, side, core, count // 4


def spot(line, side, core):
    return (line * 2 + side) * 2 + core


def meet(peers):
    barrier = pltpu.get_barrier_semaphore()
    for peer in peers:
        pl.semaphore_signal(barrier, inc=1, device_id=peer, device_id_type=MESH_ID)
    pl.semaphore_wait(barrier, len(peers))


def gather_kernel(x_ref, o_ref, local_sem, send_sem, recv_sem, *, count):
    me, line, side, core, lines = place(count)
    across = [{"fsdp": spot(lax.rem(line + s, lines), side, core)} for s in range(1, lines)]
    beside, partner = {"fsdp": spot(line, 1 - side, core)}, {"fsdp": spot(line, side, 1 - core)}
    meet(across + [beside, partner])
    sends = []

    def copy(src, shard, slot, peer):
        return pltpu.make_async_remote_copy(
            src_ref=src, dst_ref=o_ref.at[shard], send_sem=send_sem.at[slot],
            recv_sem=recv_sem.at[shard], device_id=peer, device_id_type=MESH_ID,
        )

    def send(src, shard, peer):
        made = copy(src, shard, len(sends), peer)
        made.start()
        sends.append(made)

    def arrive(shard):
        copy(o_ref.at[shard], shard, 0, partner).wait_recv()

    own = pltpu.make_async_copy(x_ref, o_ref.at[me], local_sem)
    own.start()
    for peer in across:
        send(x_ref, me, peer)
    send(x_ref, me, beside)
    send(x_ref, me, partner)
    sources = [lax.rem(line + lines - s, lines) for s in range(1, lines)]
    for source in sources:
        shard = spot(source, side, core)
        arrive(shard)
        send(o_ref.at[shard], shard, beside)
        send(o_ref.at[shard], shard, partner)
    for source in [line] + sources:
        shard = spot(source, 1 - side, core)
        arrive(shard)
        send(o_ref.at[shard], shard, partner)
    for source in [line] + sources:
        arrive(spot(source, side, 1 - core))
        arrive(spot(source, 1 - side, 1 - core))
    own.wait()
    for made in sends:
        made.wait_send()


def gather_packed(values, count):
    lines = count // 4
    full = pl.pallas_call(
        functools.partial(gather_kernel, count=count),
        out_shape=jax.ShapeDtypeStruct((count,) + values.shape, values.dtype),
        in_specs=[pl.BlockSpec(memory_space=pltpu.VMEM)],
        out_specs=pl.BlockSpec(memory_space=pltpu.VMEM),
        scratch_shapes=[
            pltpu.SemaphoreType.DMA,
            pltpu.SemaphoreType.DMA((4 * lines - 1,)),
            pltpu.SemaphoreType.DMA((count,)),
        ],
        compiler_params=pltpu.CompilerParams(collective_id=0, has_side_effects=True),
        name="gather_packed",
    )(values)
    return full


def scatter_kernel(
    fac_ref, out_ref, rest_ref, gains_ref, o_ref, part, core_in, side_in, line_in, mine, sp_in,
    core_send, core_recv, side_send, side_recv, line_send, line_recv, sp_send, sp_recv,
    *, count, shards
):
    me, line, side, core, lines = place(count)
    rank = lax.axis_index("sp")
    rows = o_ref.shape[0]
    across = [{"fsdp": spot(lax.rem(line + s, lines), side, core)} for s in range(1, lines)]
    beside, partner = {"fsdp": spot(line, 1 - side, core)}, {"fsdp": spot(line, side, 1 - core)}
    others = [{"sp": lax.rem(rank + s, shards)} for s in range(1, shards)]
    meet(across + [beside, partner] + others)
    started = []

    def copy(src, dst, send_sem, recv_sem, peer):
        return pltpu.make_async_remote_copy(
            src_ref=src, dst_ref=dst, send_sem=send_sem, recv_sem=recv_sem,
            device_id=peer, device_id_type=MESH_ID,
        )

    def send(*args):
        made = copy(*args)
        made.start()
        started.append(made)

    def load(shard):
        begin = pl.multiple_of(shard * rows, rows)
        return jnp.concatenate(
            [ref[pl.ds(begin, rows), :] for ref in (fac_ref, out_ref, rest_ref)]
            + [gains_ref[shard]],
            axis=1,
        )

    def from_core(slot):
        copy(part.at[me], core_in.at[slot], core_send.at[slot], core_recv.at[slot], partner).wait_recv()
        return core_in[slot].astype(F32)

    def from_side(slot):
        copy(part.at[me], side_in.at[slot], side_send.at[slot], side_recv.at[slot], beside).wait_recv()
        return side_in[slot].astype(F32)

    targets = [lax.rem(line + s, lines) for s in range(1, lines)] + [line]
    for which in (1 - side, side):
        for target in targets:
            shard = spot(target, which, 1 - core)
            slot = target * 2 + which
            part[shard] = load(shard)
            send(part.at[shard], core_in.at[slot], core_send.at[slot], core_recv.at[slot], partner)
    for target in targets:
        shard = spot(target, 1 - side, core)
        part[shard] = (load(shard).astype(F32) + from_core(target * 2 + 1 - side)).astype(BF16)
        send(part.at[shard], side_in.at[target], side_send.at[target], side_recv.at[target], beside)
    for s, target in enumerate(targets):
        shard = spot(target, side, core)
        total = load(shard).astype(F32) + from_core(target * 2 + side) + from_side(target)
        if s < lines - 1:
            part[shard] = total.astype(BF16)
            send(part.at[shard], line_in.at[s], line_send.at[s], line_recv.at[s], across[s])
    for s in range(lines - 1):
        copy(part.at[me], line_in.at[s], line_send.at[s], line_recv.at[s], across[s]).wait_recv()
        total = total + line_in[s].astype(F32)
    mine[...] = total.astype(BF16)
    for s, peer in enumerate(others):
        send(mine, sp_in.at[s], sp_send.at[s], sp_recv.at[s], peer)
    total = mine[...].astype(F32)
    for s, peer in enumerate(others):
        copy(mine, sp_in.at[s], sp_send.at[s], sp_recv.at[s], peer).wait_recv()
        total = total + sp_in[s].astype(F32)
    o_ref[...] = total
    for made in started:
        made.wait_send()


def scatter_packed(grad_fac, grad_out, grad_rest, grad_gains, count, shards):
    rows = grad_fac.shape[0] // count
    columns = sum(a.shape[-1] for a in (grad_fac, grad_out, grad_rest, grad_gains))
    lines = count // 4
    buffer = lambda n: pltpu.VMEM((n, rows, columns), BF16)
    sems = lambda n: pltpu.SemaphoreType.DMA((n,))
    return pl.pallas_call(
        functools.partial(scatter_kernel, count=count, shards=shards),
        out_shape=jax.ShapeDtypeStruct((rows, columns), F32),
        in_specs=[pl.BlockSpec(memory_space=pltpu.VMEM)] * 4,
        out_specs=pl.BlockSpec(memory_space=pltpu.VMEM),
        scratch_shapes=[
            buffer(count), buffer(2 * lines), buffer(lines), buffer(lines - 1),
            pltpu.VMEM((rows, columns), BF16), buffer(shards - 1),
            sems(2 * lines), sems(2 * lines), sems(lines), sems(lines),
            sems(lines - 1), sems(lines - 1), sems(shards - 1), sems(shards - 1),
        ],
        compiler_params=pltpu.CompilerParams(collective_id=1, has_side_effects=True),
        name="scatter_packed",
    )(grad_fac, grad_out, grad_rest, grad_gains)


def gather_shards(values, shards):
    me = lax.axis_index("sp")
    rows = values.shape[0]
    full = jnp.zeros((rows * shards,) + values.shape[1:], values.dtype)
    zeros = (0,) * (values.ndim - 1)
    full = lax.dynamic_update_slice(full, values, (me * rows,) + zeros)
    for shift in range(1, shards):
        part = lax.ppermute(values, "sp", [(i, (i + shift) % shards) for i in range(shards)])
        full = lax.dynamic_update_slice(full, part, (((me - shift) % shards) * rows,) + zeros)
    return full


def sum_shards(values, shards):
    if shards == 2:
        other = lax.ppermute(values, "sp", [(0, 1), (1, 0)])
        return values.astype(F32) + other.astype(F32)
    return lax.psum(values, "sp").astype(F32)


def arrange_factor(w, shards):
    heads = H // shards
    spans = ((0, RQ), (H * RQ, RK), (H * (RQ + RK), RK))
    parts = [w[:, H * RANKS :]]
    for device in range(shards):
        own = [
            w[:, base + device * heads * r : base + (device + 1) * heads * r] for base, r in spans
        ]
        parts.append(jnp.pad(jnp.concatenate(own, axis=1), ((0, 0), (0, LANES - heads * RANKS))))
    return jnp.concatenate(parts, axis=1)


def restore_factor(g, shards):
    heads = H // shards
    spans = ((0, RQ), (heads * RQ, RK), (heads * (RQ + RK), RK))
    parts = []
    for base, r in spans:
        for device in range(shards):
            begin = NB + device * LANES + base
            parts.append(g[:, begin : begin + heads * r])
    parts.append(g[:, :NB])
    return jnp.concatenate(parts, axis=1)


def local(tokens, segments, cotangent, gain_attn, w_fac, w_out, gain_ffn, w_gu, w_down, shards, count):
    me = lax.axis_index("sp")
    features = tokens.shape[2]
    heads = H // shards
    columns = heads * DH
    fac_columns = NB + shards * LANES
    own_rows = w_fac.shape[0]

    gains = jnp.concatenate([gain_attn, gain_ffn])[None]
    gains = jnp.pad(gains, ((0, own_rows - 1), (0, LANES - 2 * own_rows)))
    packed = jnp.concatenate([arrange_factor(w_fac, shards), w_out, gains], axis=1)
    packed = gather_packed(packed, count)
    gu_full = lax.all_gather(w_gu, "fsdp", axis=0, tiled=True)
    down_full = lax.all_gather(w_down, "fsdp", axis=0, tiled=True)
    gains = packed[:, 0, fac_columns + features :].astype(F32)
    gain_one = gains[:, :own_rows].reshape(1, features)
    gain_two = gains[:, own_rows : 2 * own_rows].reshape(1, features)
    packed = packed.reshape(features, packed.shape[2])
    fac_full = packed[:, :fac_columns]
    out_full = packed[:, fac_columns : fac_columns + features]

    tokens_all = gather_shards(tokens[0], shards)
    seg_all = gather_shards(segments[0], shards)
    own_left = lax.dynamic_slice_in_dim(fac_full, NB + me * LANES, LANES, 1)
    own_weights = jnp.concatenate([fac_full[:, :NB], own_left], axis=1)
    spreader = expansion(heads)
    factors, query_heads, key_heads, value_heads = heads_forward(
        tokens_all, gain_one, own_weights, spreader, columns
    )
    mixed_heads = attend_forward(query_heads, key_heads, value_heads, seg_all)
    mixed_tokens = lax.all_to_all(mixed_heads, "sp", split_axis=0, concat_axis=1, tiled=True)

    inputs = tokens[0].astype(F32)
    token_count = inputs.shape[0]
    hidden_in = inputs + product(mixed_tokens, out_full)
    normed_two = rms_norm(hidden_in, gain_two).astype(BF16)
    gate_up = product(normed_two, gu_full)
    activated = swiglu(gate_up).astype(BF16)
    gate_up, activated = lax.optimization_barrier((gate_up, activated))
    grad_out = cotangent[0].astype(F32)
    grad_low = cotangent[0]
    grad_down = weight_grad(activated, grad_low).astype(BF16)
    grad_down = lax.psum_scatter(grad_down, "fsdp", scatter_dimension=0, tiled=True)

    result = hidden_in + product(activated, down_full)
    output = result.astype(BF16)[None]

    grad_act = back_product(grad_low, down_full)
    _, pull_ffn = jax.vjp(swiglu, gate_up)
    grad_gate_up = pull_ffn(grad_act)[0].astype(BF16)
    grad_normed_two = back_product(grad_gate_up, gu_full)
    _, pull_two = jax.vjp(rms_norm, hidden_in, gain_two)
    grad_from_norm, grad_gain_two = pull_two(grad_normed_two)
    grad_hidden = grad_out + grad_from_norm
    grad_branch = grad_hidden.astype(BF16)
    grad_mixed = back_product(grad_branch, out_full).astype(BF16)
    grad_gate_up, grad_mixed = lax.optimization_barrier((grad_gate_up, grad_mixed))
    kept = grad_gate_up.shape[1] - MOVED
    grad_gu = weight_grad(normed_two, grad_gate_up[:, :kept]).astype(BF16)
    grad_gu = lax.psum_scatter(grad_gu, "fsdp", scatter_dimension=0, tiled=True)
    grad_heads = lax.all_to_all(grad_mixed, "sp", split_axis=1, concat_axis=0, tiled=True)
    grad_q, grad_k, grad_v = attend_backward(
        query_heads, key_heads, value_heads, grad_heads, seg_all
    )
    grad_parts = heads_backward(factors, spreader, grad_q, grad_k, grad_v)
    grad_gate_up, grad_branch, grad_parts = lax.optimization_barrier(
        (grad_gate_up, grad_branch, grad_parts)
    )
    grad_rest = weight_grad(normed_two, grad_gate_up[:, kept:]).astype(BF16)
    grad_wout = weight_grad(mixed_tokens, grad_branch)
    grad_parts = lax.all_to_all(
        grad_parts.reshape(shards, token_count, NB + LANES), "sp", split_axis=0, concat_axis=0
    )
    grad_right = jnp.sum(grad_parts[:, :, :NB].astype(F32), axis=0).astype(BF16)
    grad_factor = jnp.concatenate(
        [grad_right] + [grad_parts[device, :, NB:] for device in range(shards)], axis=1
    )
    normed_one = rms_norm(inputs, gain_one).astype(BF16)
    grad_fac = weight_grad(normed_one, grad_factor)
    grad_normed_one = back_product(grad_factor, fac_full)
    _, pull_one = jax.vjp(rms_norm, inputs, gain_one)
    grad_in_norm, grad_gain_one = pull_one(grad_normed_one)
    grad_tokens = (grad_hidden + grad_in_norm).reshape(1, token_count, features)

    grad_gains = jnp.concatenate(
        [grad_gain_one.reshape(count, own_rows), grad_gain_two.reshape(count, own_rows)], axis=1
    )
    grad_gains = jnp.pad(
        grad_gains[:, None], ((0, 0), (0, own_rows - 1), (0, LANES - 2 * own_rows))
    )
    grad_packed = scatter_packed(
        grad_fac.astype(BF16), grad_wout.astype(BF16), grad_rest, grad_gains.astype(BF16),
        count, shards,
    )
    grad_down = sum_shards(grad_down, shards)
    grad_gu = sum_shards(grad_gu, shards)
    tail = fac_columns + features
    gain_row = grad_packed[0, tail + MOVED :]
    grad_gu = jnp.concatenate([grad_gu, grad_packed[:, tail : tail + MOVED]], axis=1)
    return (
        output,
        grad_tokens,
        gain_row[:own_rows],
        restore_factor(grad_packed[:, :fac_columns], shards),
        grad_packed[:, fac_columns : fac_columns + features],
        gain_row[own_rows : 2 * own_rows],
        grad_gu,
        grad_down,
    )


def solution(mesh):
    in_specs = (
        P("fsdp", "sp", None),
        P("fsdp", "sp"),
        P("fsdp", "sp", None),
        P("fsdp"),
        P("fsdp", None),
        P("fsdp", None),
        P("fsdp"),
        P("fsdp", None),
        P("fsdp", None),
    )
    out_specs = (
        P("fsdp", "sp", None),
        P("fsdp", "sp", None),
        P("fsdp"),
        P("fsdp", None),
        P("fsdp", None),
        P("fsdp"),
        P("fsdp", None),
        P("fsdp", None),
    )

    def body(*args):
        return local(*args, shards=mesh.shape["sp"], count=mesh.shape["fsdp"])

    return jax.shard_map(body, mesh=mesh, in_specs=in_specs, out_specs=out_specs, check_vma=False)
```

```python
import functools

import jax
import jax.numpy as jnp
from jax import lax
from jax.experimental import pallas as pl
from jax.experimental.pallas import tpu as pltpu
from jax.sharding import PartitionSpec as P


H = 16
DH = 64
RQ = 6
RK = 2
FF = 2816
LANES = 128
NB = (RQ + 2 * RK) * DH
RANKS = RQ + 2 * RK
MOVED = 1024

EPSILON = 1e-06
NEG = -1e30
F32 = jnp.float32
BF16 = jnp.bfloat16


def rms_norm(values, gain_row):
    factor = lax.rsqrt(jnp.mean(values * values, axis=-1, keepdims=True) + EPSILON)
    return values * factor * gain_row


def swiglu(gate_up):
    return jax.nn.silu(gate_up[:, :FF]) * gate_up[:, FF:]


def product(left, right):
    return jnp.dot(left, right, preferred_element_type=F32)


def weight_grad(left, right):
    return jnp.einsum("ta,tb->ab", left, right, preferred_element_type=F32)


def back_product(grad_rows, weight):
    return jnp.einsum("tb,ab->ta", grad_rows, weight, preferred_element_type=F32)


def dot_nt(a, b):
    return lax.dot_general(a, b, (((1,), (1,)), ((), ())), preferred_element_type=F32)


def dot_tn(a, b):
    return lax.dot_general(a, b, (((0,), (0,)), ((), ())), preferred_element_type=F32)


def band_start(index, block, width):
    return pl.multiple_of(jnp.maximum(index * block - (width - block), 0), LANES)


def band_bias(index, start, seg_col, seg_row, block, width):
    rows = index * block + lax.broadcasted_iota(jnp.int32, (block, width), 0)
    cols = start + lax.broadcasted_iota(jnp.int32, (block, width), 1)
    keep = (seg_col == seg_row) & (cols <= rows)
    return jnp.where(keep, 0.0, NEG)


def half_masks(scale):
    lane = lax.broadcasted_iota(jnp.int32, (1, LANES), 1)
    low = jnp.where(lane < DH, scale, 0.0).astype(BF16)
    high = jnp.where(lane < DH, 0.0, scale).astype(BF16)
    return low, high


def split_pair(values, masks):
    return jnp.concatenate([values * masks[0], values * masks[1]], axis=0)


def attend_forward_kernel(q_ref, k_ref, v_ref, segc_ref, segr_ref, o_ref, *, block, width):
    index = pl.program_id(0)
    start = band_start(index, block, width)
    bias = band_bias(index, start, segc_ref[...], segr_ref[:, pl.ds(start, width)], block, width)
    bias = jnp.concatenate([bias, bias], axis=0)
    masks = half_masks(DH ** (-0.5))
    first = lax.broadcasted_iota(jnp.int32, (block, LANES), 1) < DH
    for pair in range(q_ref.shape[1] // LANES):
        lanes = slice(pair * LANES, (pair + 1) * LANES)
        queries = split_pair(q_ref[:, lanes], masks)
        keys = k_ref[pl.ds(start, width), lanes]
        values = v_ref[pl.ds(start, width), lanes]
        scores = dot_nt(queries, keys) + bias
        exponent = jnp.exp(scores - jnp.max(scores, axis=-1, keepdims=True))
        inverse = 1.0 / jnp.sum(exponent, axis=-1, keepdims=True)
        probs = (exponent * inverse).astype(BF16)
        mixed = product(probs, values)
        o_ref[:, lanes] = jnp.where(first, mixed[:block], mixed[block:]).astype(BF16)


def attend_backward_kernel(
    q_ref, k_ref, v_ref, g_ref, segc_ref, segr_ref, dq_ref, dk_ref, dv_ref, dk_acc, dv_acc,
    *, block, width
):
    index = pl.program_id(0)
    start = band_start(index, block, width)
    scaling = DH ** (-0.5)

    @pl.when(index == 0)
    def _():
        dk_acc[...] = jnp.zeros_like(dk_acc)
        dv_acc[...] = jnp.zeros_like(dv_acc)

    bias = band_bias(index, start, segc_ref[...], segr_ref[:, pl.ds(start, width)], block, width)
    bias = jnp.concatenate([bias, bias], axis=0)
    scale_masks = half_masks(scaling)
    unit_masks = half_masks(1.0)
    first = lax.broadcasted_iota(jnp.int32, (block, LANES), 1) < DH
    window = pl.ds(start, width)
    for pair in range(q_ref.shape[1] // LANES):
        lanes = slice(pair * LANES, (pair + 1) * LANES)
        queries = split_pair(q_ref[:, lanes], scale_masks)
        grads = split_pair(g_ref[:, lanes], unit_masks)
        keys = k_ref[window, lanes]
        values = v_ref[window, lanes]
        scores = dot_nt(queries, keys) + bias
        exponent = jnp.exp(scores - jnp.max(scores, axis=-1, keepdims=True))
        inverse = 1.0 / jnp.sum(exponent, axis=-1, keepdims=True)
        probs = exponent * inverse
        grad_probs = dot_nt(grads, values)
        inner = jnp.sum(probs * grad_probs, axis=-1, keepdims=True)
        grad_scores = (probs * (grad_probs - inner)).astype(BF16)
        grad_q = product(grad_scores, keys) * scaling
        dq_ref[:, lanes] = jnp.where(first, grad_q[:block], grad_q[block:]).astype(BF16)
        dk_acc[window, lanes] += dot_tn(grad_scores, queries)
        dv_acc[window, lanes] += dot_tn(probs.astype(BF16), grads)

    @pl.when(index == pl.num_programs(0) - 1)
    def _():
        dk_ref[...] = dk_acc[...].astype(BF16)
        dv_ref[...] = dv_acc[...].astype(BF16)


def attention_specs(length, columns):
    block = LANES
    width = min(length // 4 + block, length)
    whole = pl.BlockSpec((length, columns), lambda i: (0, 0))
    rows = pl.BlockSpec((block, columns), lambda i: (i, 0))
    seg_col = pl.BlockSpec((block, 1), lambda i: (i, 0))
    seg_row = pl.BlockSpec((1, length), lambda i: (0, 0))
    return block, width, whole, rows, seg_col, seg_row


def attend_forward(queries, keys, values, seg_all):
    length, columns = queries.shape
    block, width, whole, rows, seg_col, seg_row = attention_specs(length, columns)
    work = length * width * columns
    return pl.pallas_call(
        functools.partial(attend_forward_kernel, block=block, width=width),
        grid=(length // block,),
        in_specs=[rows, whole, whole, seg_col, seg_row],
        out_specs=rows,
        out_shape=jax.ShapeDtypeStruct((length, columns), BF16),
        cost_estimate=pl.CostEstimate(
            flops=16 * work, bytes_accessed=8 * length * columns, transcendentals=work // DH
        ),
        name="attend_forward",
    )(queries, keys, values, seg_all.reshape(length, 1), seg_all.reshape(1, length))


def attend_backward(queries, keys, values, grads, seg_all):
    length, columns = queries.shape
    block, width, whole, rows, seg_col, seg_row = attention_specs(length, columns)
    work = length * width * columns
    shape = jax.ShapeDtypeStruct((length, columns), BF16)
    return pl.pallas_call(
        functools.partial(attend_backward_kernel, block=block, width=width),
        grid=(length // block,),
        in_specs=[rows, whole, whole, rows, seg_col, seg_row],
        out_specs=[rows, whole, whole],
        out_shape=[shape, shape, shape],
        scratch_shapes=[pltpu.VMEM((length, columns), F32), pltpu.VMEM((length, columns), F32)],
        cost_estimate=pl.CostEstimate(
            flops=40 * work, bytes_accessed=14 * length * columns, transcendentals=work // DH
        ),
        name="attend_backward",
    )(queries, keys, values, grads, seg_all.reshape(length, 1), seg_all.reshape(1, length))


def expansion(heads):
    rows = lax.broadcasted_iota(jnp.int32, (2 * LANES, RANKS * heads * DH), 0) % LANES
    cols = lax.broadcasted_iota(jnp.int32, (2 * LANES, RANKS * heads * DH), 1)
    rank, head = cols // (heads * DH), (cols % (heads * DH)) // DH
    in_k = heads * RQ + head * RK + rank - RQ
    in_v = heads * (RQ + RK) + head * RK + rank - RQ - RK
    source = jnp.where(
        rank < RQ, head * RQ + rank, jnp.where(rank < RQ + RK, in_k, in_v)
    )
    return (rows == source).astype(BF16)


def high_low(values):
    high = values.astype(BF16)
    return high, (values - high.astype(F32)).astype(BF16)


def doubled(factor, rank, first):
    pair = factor[:, (rank // 2) * LANES : (rank // 2 + 1) * LANES]
    turned = pltpu.roll(pair, DH, 1)
    return jnp.where(first, pair, turned) if rank % 2 == 0 else jnp.where(first, turned, pair)


GROUPS = ((0, RQ), (RQ, RK), (RQ + RK, RK))


def heads_forward_kernel(x_ref, gain_ref, w_ref, e_ref, f_ref, q_ref, k_ref, v_ref):
    normed = rms_norm(x_ref[...].astype(F32), gain_ref[...]).astype(BF16)
    factor = product(normed, w_ref[...])
    f_ref[...] = factor
    spread = jnp.concatenate(high_low(factor[:, NB:]), axis=1)
    rows, columns = q_ref.shape
    first = lax.broadcasted_iota(jnp.int32, (rows, LANES), 1) < DH
    for (base, ranks), out_ref in zip(GROUPS, (q_ref, k_ref, v_ref)):
        total = None
        for rank in range(base, base + ranks):
            left = product(spread, e_ref[:, rank * columns : (rank + 1) * columns])
            right = jnp.concatenate([doubled(factor, rank, first)] * (columns // LANES), axis=1)
            total = left * right if total is None else total + left * right
        out_ref[...] = (total * (1.0 / ranks)).astype(BF16)


def heads_backward_kernel(f_ref, e_ref, dq_ref, dk_ref, dv_ref, g_ref):
    factor = f_ref[...]
    spread = jnp.concatenate(high_low(factor[:, NB:]), axis=1)
    rows, columns = dq_ref.shape
    first = lax.broadcasted_iota(jnp.int32, (rows, LANES), 1) < DH
    left_total = jnp.zeros((rows, LANES), F32)
    folded = []
    for (base, ranks), grad_ref in zip(GROUPS, (dq_ref, dk_ref, dv_ref)):
        grad = grad_ref[...].astype(F32) * (1.0 / ranks)
        for rank in range(base, base + ranks):
            ones = e_ref[:, rank * columns : (rank + 1) * columns]
            weighted = product(spread, ones) * grad
            right_grad = weighted[:, :LANES]
            for chunk in range(1, columns // LANES):
                right_grad = right_grad + weighted[:, chunk * LANES : (chunk + 1) * LANES]
            folded.append(right_grad + pltpu.roll(right_grad, DH, 1))
            right = jnp.concatenate([doubled(factor, rank, first)] * (columns // LANES), axis=1)
            high, low = high_low(grad * right)
            left_total = left_total + dot_nt(high, ones[:LANES]) + dot_nt(low, ones[:LANES])
    for pair in range(RANKS // 2):
        g_ref[:, pair * LANES : (pair + 1) * LANES] = jnp.where(
            first, folded[2 * pair], folded[2 * pair + 1]
        ).astype(BF16)
    g_ref[:, NB:] = left_total.astype(BF16)


HEAD_ROWS = 256


def heads_forward(tokens, gain_row, weights, spreader, columns):
    length, width = tokens.shape
    rows = min(HEAD_ROWS, length)
    block = lambda n: pl.BlockSpec((rows, n), lambda i: (i, 0))
    fixed = lambda a: pl.BlockSpec(a.shape, lambda i: (0, 0))
    head = jax.ShapeDtypeStruct((length, columns), BF16)
    return pl.pallas_call(
        heads_forward_kernel,
        grid=(length // rows,),
        in_specs=[block(width), fixed(gain_row), fixed(weights), fixed(spreader)],
        out_specs=[block(NB + LANES)] + [block(columns)] * 3,
        out_shape=[jax.ShapeDtypeStruct((length, NB + LANES), F32), head, head, head],
        name="heads_forward",
    )(tokens, gain_row, weights, spreader)


def heads_backward(factors, spreader, grad_q, grad_k, grad_v):
    length, columns = grad_q.shape
    rows = min(HEAD_ROWS, length)
    block = lambda n: pl.BlockSpec((rows, n), lambda i: (i, 0))
    return pl.pallas_call(
        heads_backward_kernel,
        grid=(length // rows,),
        in_specs=[
            block(NB + LANES), pl.BlockSpec(spreader.shape, lambda i: (0, 0)),
            block(columns), block(columns), block(columns),
        ],
        out_specs=block(NB + LANES),
        out_shape=jax.ShapeDtypeStruct((length, NB + LANES), BF16),
        name="heads_backward",
    )(factors, spreader, grad_q, grad_k, grad_v)


MESH_ID = pl.DeviceIdType.MESH


def place(count):
    me = lax.axis_index("fsdp")
    line, side, core = me // 4, (me // 2) % 2, me % 2
    return me, line, side, core, count // 4


def spot(line, side, core):
    return (line * 2 + side) * 2 + core


def meet(peers):
    barrier = pltpu.get_barrier_semaphore()
    for peer in peers:
        pl.semaphore_signal(barrier, inc=1, device_id=peer, device_id_type=MESH_ID)
    pl.semaphore_wait(barrier, len(peers))


def halves(columns):
    rank = lax.axis_index("sp")
    half = columns // 2
    own = pl.ds(pl.multiple_of(rank * half, LANES), half)
    other = pl.ds(pl.multiple_of((1 - rank) * half, LANES), half)
    return {"sp": 1 - rank}, own, other


def gather_kernel(x_ref, o_ref, local_sem, send_sem, recv_sem, line_sem, mate_sem, *, count, split):
    me, line, side, core, lines = place(count)
    across = [{"fsdp": spot(lax.rem(line + s, lines), side, core)} for s in range(1, lines)]
    beside, partner = {"fsdp": spot(line, 1 - side, core)}, {"fsdp": spot(line, side, 1 - core)}
    if split:
        mate, span, _ = halves(x_ref.shape[1])
    else:
        mate, span = None, slice(None)
    meet(across + [beside, partner] + ([mate] if split else []))
    sends = []

    def copy(src, dst, slot, sem, peer):
        return pltpu.make_async_remote_copy(
            src_ref=src, dst_ref=dst, send_sem=send_sem.at[slot], recv_sem=sem,
            device_id=peer, device_id_type=MESH_ID,
        )

    def send(src, dst, sem, peer):
        made = copy(src, dst, len(sends), sem, peer)
        made.start()
        sends.append(made)

    def forward(src, shard, peer):
        send(src, o_ref.at[shard], recv_sem.at[shard], peer)

    def arrive(ref, sem):
        copy(ref, ref, 0, sem, partner).wait_recv()

    own = pltpu.make_async_copy(x_ref, o_ref.at[me], local_sem)
    own.start()
    for peer in across:
        send(x_ref.at[:, span], o_ref.at[me, :, span], line_sem.at[me], peer)
    forward(x_ref, me, beside)
    forward(x_ref, me, partner)
    sources = [lax.rem(line + lines - s, lines) for s in range(1, lines)]
    if split:
        for source in sources:
            shard = spot(source, side, core)
            part = o_ref.at[shard, :, span]
            arrive(part, line_sem.at[shard])
            send(part, part, mate_sem.at[shard], mate)
    for source in sources:
        shard = spot(source, side, core)
        arrive(o_ref.at[shard, :, span], (mate_sem if split else line_sem).at[shard])
        forward(o_ref.at[shard], shard, beside)
        forward(o_ref.at[shard], shard, partner)
    for source in [line] + sources:
        shard = spot(source, 1 - side, core)
        arrive(o_ref.at[shard], recv_sem.at[shard])
        forward(o_ref.at[shard], shard, partner)
    for source in [line] + sources:
        for which in (side, 1 - side):
            shard = spot(source, which, 1 - core)
            arrive(o_ref.at[shard], recv_sem.at[shard])
    own.wait()
    for made in sends:
        made.wait_send()


def gather_packed(values, count, shards):
    lines = count // 4
    split = shards == 2
    sems = lambda n: pltpu.SemaphoreType.DMA((n,))
    return pl.pallas_call(
        functools.partial(gather_kernel, count=count, split=split),
        out_shape=jax.ShapeDtypeStruct((count,) + values.shape, values.dtype),
        in_specs=[pl.BlockSpec(memory_space=pltpu.VMEM)],
        out_specs=pl.BlockSpec(memory_space=pltpu.VMEM),
        scratch_shapes=[
            pltpu.SemaphoreType.DMA, sems(5 * lines - 2 if split else 4 * lines - 1),
            sems(count), sems(count), sems(count),
        ],
        compiler_params=pltpu.CompilerParams(collective_id=0, has_side_effects=True),
        name="gather_packed",
    )(values)


def scatter_kernel(
    fac_ref, out_ref, rest_ref, gains_ref, o_ref, part, core_in, side_in, line_in, mine, sp_in, last_in,
    core_send, core_recv, side_send, side_recv, line_send, line_recv, sp_send, sp_recv,
    last_send, last_recv,
    *, count, shards
):
    me, line, side, core, lines = place(count)
    rank = lax.axis_index("sp")
    rows = o_ref.shape[0]
    across = [{"fsdp": spot(lax.rem(line + s, lines), side, core)} for s in range(1, lines)]
    beside, partner = {"fsdp": spot(line, 1 - side, core)}, {"fsdp": spot(line, side, 1 - core)}
    others = [{"sp": lax.rem(rank + s, shards)} for s in range(1, shards)]
    meet(across + [beside, partner] + others)
    started = []

    def copy(src, dst, send_sem, recv_sem, peer):
        return pltpu.make_async_remote_copy(
            src_ref=src, dst_ref=dst, send_sem=send_sem, recv_sem=recv_sem,
            device_id=peer, device_id_type=MESH_ID,
        )

    def send(*args):
        made = copy(*args)
        made.start()
        started.append(made)

    def load(shard):
        begin = pl.multiple_of(shard * rows, rows)
        return jnp.concatenate(
            [ref[pl.ds(begin, rows), :] for ref in (fac_ref, out_ref, rest_ref)]
            + [gains_ref[shard]],
            axis=1,
        )

    def from_core(slot):
        copy(part.at[me], core_in.at[slot], core_send.at[slot], core_recv.at[slot], partner).wait_recv()
        return core_in[slot].astype(F32)

    def from_side(slot):
        copy(part.at[me], side_in.at[slot], side_send.at[slot], side_recv.at[slot], beside).wait_recv()
        return side_in[slot].astype(F32)

    targets = [lax.rem(line + s, lines) for s in range(1, lines)] + [line]
    for which in (1 - side, side):
        for target in targets:
            shard = spot(target, which, 1 - core)
            slot = target * 2 + which
            part[shard] = load(shard)
            send(part.at[shard], core_in.at[slot], core_send.at[slot], core_recv.at[slot], partner)
    for target in targets:
        shard = spot(target, 1 - side, core)
        part[shard] = (load(shard).astype(F32) + from_core(target * 2 + 1 - side)).astype(BF16)
        send(part.at[shard], side_in.at[target], side_send.at[target], side_recv.at[target], beside)

    def whole_sum(target):
        shard = spot(target, side, core)
        return load(shard).astype(F32) + from_core(target * 2 + side) + from_side(target)

    if shards == 2:
        mate, span, rest = halves(o_ref.shape[1])
        for s, target in enumerate(targets):
            shard = spot(target, side, core)
            part[shard] = whole_sum(target).astype(BF16)
            send(part.at[shard, :, rest], sp_in.at[s], sp_send.at[s], sp_recv.at[s], mate)
        for s, target in enumerate(targets):
            shard = spot(target, side, core)
            copy(part.at[me, :, rest], sp_in.at[s], sp_send.at[s], sp_recv.at[s], mate).wait_recv()
            total = part[shard, :, span].astype(F32) + sp_in[s].astype(F32)
            if s < lines - 1:
                mine[s] = total.astype(BF16)
                send(mine.at[s], line_in.at[s], line_send.at[s], line_recv.at[s], across[s])
        for s in range(lines - 1):
            copy(mine.at[s], line_in.at[s], line_send.at[s], line_recv.at[s], across[s]).wait_recv()
            total = total + line_in[s].astype(F32)
        mine[lines - 1] = total.astype(BF16)
        send(mine.at[lines - 1], last_in, last_send, last_recv, mate)
        o_ref[:, span] = mine[lines - 1].astype(F32)
        copy(mine.at[lines - 1], last_in, last_send, last_recv, mate).wait_recv()
        o_ref[:, rest] = last_in[...].astype(F32)
    else:
        for s, target in enumerate(targets):
            total = whole_sum(target)
            if s < lines - 1:
                shard = spot(target, side, core)
                part[shard] = total.astype(BF16)
                send(part.at[shard], line_in.at[s], line_send.at[s], line_recv.at[s], across[s])
        for s in range(lines - 1):
            copy(part.at[me], line_in.at[s], line_send.at[s], line_recv.at[s], across[s]).wait_recv()
            total = total + line_in[s].astype(F32)
        mine[0] = total.astype(BF16)
        for s, peer in enumerate(others):
            send(mine.at[0], sp_in.at[s], sp_send.at[s], sp_recv.at[s], peer)
        total = mine[0].astype(F32)
        for s, peer in enumerate(others):
            copy(mine.at[0], sp_in.at[s], sp_send.at[s], sp_recv.at[s], peer).wait_recv()
            total = total + sp_in[s].astype(F32)
        o_ref[...] = total
    for made in started:
        made.wait_send()


def scatter_packed(grad_fac, grad_out, grad_rest, grad_gains, count, shards):
    rows = grad_fac.shape[0] // count
    columns = sum(a.shape[-1] for a in (grad_fac, grad_out, grad_rest, grad_gains))
    lines = count // 4
    split = shards == 2
    span = columns // 2 if split else columns
    passes = lines if split else shards - 1
    buffer = lambda n: pltpu.VMEM((n, rows, columns), BF16)
    narrow = lambda n: pltpu.VMEM((n, rows, span), BF16)
    sems = lambda n: pltpu.SemaphoreType.DMA((n,))
    return pl.pallas_call(
        functools.partial(scatter_kernel, count=count, shards=shards),
        out_shape=jax.ShapeDtypeStruct((rows, columns), F32),
        in_specs=[pl.BlockSpec(memory_space=pltpu.VMEM)] * 4,
        out_specs=pl.BlockSpec(memory_space=pltpu.VMEM),
        scratch_shapes=[
            buffer(count), buffer(2 * lines), buffer(lines), narrow(lines - 1),
            narrow(lines if split else 1), narrow(passes), pltpu.VMEM((rows, span), BF16),
            sems(2 * lines), sems(2 * lines), sems(lines), sems(lines),
            sems(lines - 1), sems(lines - 1), sems(passes), sems(passes),
            pltpu.SemaphoreType.DMA, pltpu.SemaphoreType.DMA,
        ],
        compiler_params=pltpu.CompilerParams(collective_id=1, has_side_effects=True),
        name="scatter_packed",
    )(grad_fac, grad_out, grad_rest, grad_gains)


def gather_shards(values, shards):
    me = lax.axis_index("sp")
    rows = values.shape[0]
    full = jnp.zeros((rows * shards,) + values.shape[1:], values.dtype)
    zeros = (0,) * (values.ndim - 1)
    full = lax.dynamic_update_slice(full, values, (me * rows,) + zeros)
    for shift in range(1, shards):
        part = lax.ppermute(values, "sp", [(i, (i + shift) % shards) for i in range(shards)])
        full = lax.dynamic_update_slice(full, part, (((me - shift) % shards) * rows,) + zeros)
    return full


def sum_shards(values, shards):
    if shards == 2:
        other = lax.ppermute(values, "sp", [(0, 1), (1, 0)])
        return values.astype(F32) + other.astype(F32)
    return lax.psum(values, "sp").astype(F32)


def arrange_factor(w, shards):
    heads = H // shards
    spans = ((0, RQ), (H * RQ, RK), (H * (RQ + RK), RK))
    parts = [w[:, H * RANKS :]]
    for device in range(shards):
        own = [
            w[:, base + device * heads * r : base + (device + 1) * heads * r] for base, r in spans
        ]
        parts.append(jnp.pad(jnp.concatenate(own, axis=1), ((0, 0), (0, LANES - heads * RANKS))))
    return jnp.concatenate(parts, axis=1)


def restore_factor(g, shards):
    heads = H // shards
    spans = ((0, RQ), (heads * RQ, RK), (heads * (RQ + RK), RK))
    parts = []
    for base, r in spans:
        for device in range(shards):
            begin = NB + device * LANES + base
            parts.append(g[:, begin : begin + heads * r])
    parts.append(g[:, :NB])
    return jnp.concatenate(parts, axis=1)


def local(tokens, segments, cotangent, gain_attn, w_fac, w_out, gain_ffn, w_gu, w_down, shards, count):
    me = lax.axis_index("sp")
    features = tokens.shape[2]
    heads = H // shards
    columns = heads * DH
    fac_columns = NB + shards * LANES
    own_rows = w_fac.shape[0]

    gains = jnp.concatenate([gain_attn, gain_ffn])[None]
    gains = jnp.pad(gains, ((0, own_rows - 1), (0, LANES - 2 * own_rows)))
    packed = jnp.concatenate([arrange_factor(w_fac, shards), w_out, gains], axis=1)
    packed = gather_packed(packed, count, shards)
    gu_full = lax.all_gather(w_gu, "fsdp", axis=0, tiled=True)
    down_full = lax.all_gather(w_down, "fsdp", axis=0, tiled=True)
    gains = packed[:, 0, fac_columns + features :].astype(F32)
    gain_one = gains[:, :own_rows].reshape(1, features)
    gain_two = gains[:, own_rows : 2 * own_rows].reshape(1, features)
    packed = packed.reshape(features, packed.shape[2])
    fac_full = packed[:, :fac_columns]
    out_full = packed[:, fac_columns : fac_columns + features]

    tokens_all = gather_shards(tokens[0], shards)
    seg_all = gather_shards(segments[0], shards)
    own_left = lax.dynamic_slice_in_dim(fac_full, NB + me * LANES, LANES, 1)
    own_weights = jnp.concatenate([fac_full[:, :NB], own_left], axis=1)
    spreader = expansion(heads)
    factors, query_heads, key_heads, value_heads = heads_forward(
        tokens_all, gain_one, own_weights, spreader, columns
    )
    mixed_heads = attend_forward(query_heads, key_heads, value_heads, seg_all)
    mixed_tokens = lax.all_to_all(mixed_heads, "sp", split_axis=0, concat_axis=1, tiled=True)

    inputs = tokens[0].astype(F32)
    token_count = inputs.shape[0]
    hidden_in = inputs + product(mixed_tokens, out_full)
    normed_two = rms_norm(hidden_in, gain_two).astype(BF16)
    gate_up = product(normed_two, gu_full)
    activated = swiglu(gate_up).astype(BF16)
    gate_up, activated = lax.optimization_barrier((gate_up, activated))
    grad_out = cotangent[0].astype(F32)
    grad_low = cotangent[0]
    grad_down = weight_grad(activated, grad_low).astype(BF16)
    grad_down = lax.psum_scatter(grad_down, "fsdp", scatter_dimension=0, tiled=True)

    result = hidden_in + product(activated, down_full)
    output = result.astype(BF16)[None]

    grad_act = back_product(grad_low, down_full)
    _, pull_ffn = jax.vjp(swiglu, gate_up)
    grad_gate_up = pull_ffn(grad_act)[0].astype(BF16)
    grad_normed_two = back_product(grad_gate_up, gu_full)
    _, pull_two = jax.vjp(rms_norm, hidden_in, gain_two)
    grad_from_norm, grad_gain_two = pull_two(grad_normed_two)
    grad_hidden = grad_out + grad_from_norm
    grad_branch = grad_hidden.astype(BF16)
    grad_mixed = back_product(grad_branch, out_full).astype(BF16)
    grad_gate_up, grad_mixed = lax.optimization_barrier((grad_gate_up, grad_mixed))
    kept = grad_gate_up.shape[1] - MOVED
    grad_gu = weight_grad(normed_two, grad_gate_up[:, :kept]).astype(BF16)
    grad_gu = lax.psum_scatter(grad_gu, "fsdp", scatter_dimension=0, tiled=True)
    grad_heads = lax.all_to_all(grad_mixed, "sp", split_axis=1, concat_axis=0, tiled=True)
    grad_q, grad_k, grad_v = attend_backward(
        query_heads, key_heads, value_heads, grad_heads, seg_all
    )
    grad_parts = heads_backward(factors, spreader, grad_q, grad_k, grad_v)
    grad_gate_up, grad_branch, grad_parts = lax.optimization_barrier(
        (grad_gate_up, grad_branch, grad_parts)
    )
    grad_rest = weight_grad(normed_two, grad_gate_up[:, kept:]).astype(BF16)
    grad_wout = weight_grad(mixed_tokens, grad_branch)
    grad_parts = lax.all_to_all(
        grad_parts.reshape(shards, token_count, NB + LANES), "sp", split_axis=0, concat_axis=0
    )
    grad_right = jnp.sum(grad_parts[:, :, :NB].astype(F32), axis=0).astype(BF16)
    grad_factor = jnp.concatenate(
        [grad_right] + [grad_parts[device, :, NB:] for device in range(shards)], axis=1
    )
    normed_one = rms_norm(inputs, gain_one).astype(BF16)
    grad_fac = weight_grad(normed_one, grad_factor)
    grad_normed_one = back_product(grad_factor, fac_full)
    _, pull_one = jax.vjp(rms_norm, inputs, gain_one)
    grad_in_norm, grad_gain_one = pull_one(grad_normed_one)
    grad_tokens = (grad_hidden + grad_in_norm).reshape(1, token_count, features)

    grad_gains = jnp.concatenate(
        [grad_gain_one.reshape(count, own_rows), grad_gain_two.reshape(count, own_rows)], axis=1
    )
    grad_gains = jnp.pad(
        grad_gains[:, None], ((0, 0), (0, own_rows - 1), (0, LANES - 2 * own_rows))
    )
    grad_packed = scatter_packed(
        grad_fac.astype(BF16), grad_wout.astype(BF16), grad_rest, grad_gains.astype(BF16),
        count, shards,
    )
    grad_down = sum_shards(grad_down, shards)
    grad_gu = sum_shards(grad_gu, shards)
    tail = fac_columns + features
    gain_row = grad_packed[0, tail + MOVED :]
    grad_gu = jnp.concatenate([grad_gu, grad_packed[:, tail : tail + MOVED]], axis=1)
    return (
        output,
        grad_tokens,
        gain_row[:own_rows],
        restore_factor(grad_packed[:, :fac_columns], shards),
        grad_packed[:, fac_columns : fac_columns + features],
        gain_row[own_rows : 2 * own_rows],
        grad_gu,
        grad_down,
    )


def solution(mesh):
    in_specs = (
        P("fsdp", "sp", None),
        P("fsdp", "sp"),
        P("fsdp", "sp", None),
        P("fsdp"),
        P("fsdp", None),
        P("fsdp", None),
        P("fsdp"),
        P("fsdp", None),
        P("fsdp", None),
    )
    out_specs = (
        P("fsdp", "sp", None),
        P("fsdp", "sp", None),
        P("fsdp"),
        P("fsdp", None),
        P("fsdp", None),
        P("fsdp"),
        P("fsdp", None),
        P("fsdp", None),
    )

    def body(*args):
        return local(*args, shards=mesh.shape["sp"], count=mesh.shape["fsdp"])

    return jax.shard_map(body, mesh=mesh, in_specs=in_specs, out_specs=out_specs, check_vma=False)
```

```python
import functools

import jax
import jax.numpy as jnp
from jax import lax
from jax.experimental import pallas as pl
from jax.experimental.pallas import tpu as pltpu
from jax.sharding import PartitionSpec as P


H = 16
DH = 64
RQ = 6
RK = 2
FF = 2816
LANES = 128
NB = (RQ + 2 * RK) * DH
RANKS = RQ + 2 * RK
MOVED = 1280

EPSILON = 1e-06
NEG = -1e30
F32 = jnp.float32
BF16 = jnp.bfloat16


def rms_norm(values, gain_row):
    factor = lax.rsqrt(jnp.mean(values * values, axis=-1, keepdims=True) + EPSILON)
    return values * factor * gain_row


def swiglu(gate_up):
    return jax.nn.silu(gate_up[:, :FF]) * gate_up[:, FF:]


def product(left, right):
    return jnp.dot(left, right, preferred_element_type=F32)


def weight_grad(left, right):
    return jnp.einsum("ta,tb->ab", left, right, preferred_element_type=F32)


def back_product(grad_rows, weight):
    return jnp.einsum("tb,ab->ta", grad_rows, weight, preferred_element_type=F32)


def dot_nt(a, b):
    return lax.dot_general(a, b, (((1,), (1,)), ((), ())), preferred_element_type=F32)


def dot_tn(a, b):
    return lax.dot_general(a, b, (((0,), (0,)), ((), ())), preferred_element_type=F32)


def band_start(index, block, width):
    return pl.multiple_of(jnp.maximum(index * block - (width - block), 0), LANES)


def band_bias(index, start, seg_col, seg_row, block, width):
    rows = index * block + lax.broadcasted_iota(jnp.int32, (block, width), 0)
    cols = start + lax.broadcasted_iota(jnp.int32, (block, width), 1)
    keep = (seg_col == seg_row) & (cols <= rows)
    return jnp.where(keep, 0.0, NEG)


def half_masks(scale):
    lane = lax.broadcasted_iota(jnp.int32, (1, LANES), 1)
    low = jnp.where(lane < DH, scale, 0.0).astype(BF16)
    high = jnp.where(lane < DH, 0.0, scale).astype(BF16)
    return low, high


def split_pair(values, masks):
    return jnp.concatenate([values * masks[0], values * masks[1]], axis=0)


def attend_forward_kernel(q_ref, k_ref, v_ref, segc_ref, segr_ref, o_ref, *, block, width):
    index = pl.program_id(0)
    start = band_start(index, block, width)
    bias = band_bias(index, start, segc_ref[...], segr_ref[:, pl.ds(start, width)], block, width)
    bias = jnp.concatenate([bias, bias], axis=0)
    masks = half_masks(DH ** (-0.5))
    first = lax.broadcasted_iota(jnp.int32, (block, LANES), 1) < DH
    for pair in range(q_ref.shape[1] // LANES):
        lanes = slice(pair * LANES, (pair + 1) * LANES)
        queries = split_pair(q_ref[:, lanes], masks)
        keys = k_ref[pl.ds(start, width), lanes]
        values = v_ref[pl.ds(start, width), lanes]
        scores = dot_nt(queries, keys) + bias
        exponent = jnp.exp(scores - jnp.max(scores, axis=-1, keepdims=True))
        inverse = 1.0 / jnp.sum(exponent, axis=-1, keepdims=True)
        probs = (exponent * inverse).astype(BF16)
        mixed = product(probs, values)
        o_ref[:, lanes] = jnp.where(first, mixed[:block], mixed[block:]).astype(BF16)


def attend_backward_kernel(
    q_ref, k_ref, v_ref, g_ref, segc_ref, segr_ref, dq_ref, dk_ref, dv_ref, dk_acc, dv_acc,
    *, block, width
):
    index = pl.program_id(0)
    start = band_start(index, block, width)
    scaling = DH ** (-0.5)

    @pl.when(index == 0)
    def _():
        dk_acc[...] = jnp.zeros_like(dk_acc)
        dv_acc[...] = jnp.zeros_like(dv_acc)

    bias = band_bias(index, start, segc_ref[...], segr_ref[:, pl.ds(start, width)], block, width)
    bias = jnp.concatenate([bias, bias], axis=0)
    scale_masks = half_masks(scaling)
    unit_masks = half_masks(1.0)
    first = lax.broadcasted_iota(jnp.int32, (block, LANES), 1) < DH
    window = pl.ds(start, width)
    for pair in range(q_ref.shape[1] // LANES):
        lanes = slice(pair * LANES, (pair + 1) * LANES)
        queries = split_pair(q_ref[:, lanes], scale_masks)
        grads = split_pair(g_ref[:, lanes], unit_masks)
        keys = k_ref[window, lanes]
        values = v_ref[window, lanes]
        scores = dot_nt(queries, keys) + bias
        exponent = jnp.exp(scores - jnp.max(scores, axis=-1, keepdims=True))
        inverse = 1.0 / jnp.sum(exponent, axis=-1, keepdims=True)
        probs = exponent * inverse
        grad_probs = dot_nt(grads, values)
        inner = jnp.sum(probs * grad_probs, axis=-1, keepdims=True)
        grad_scores = (probs * (grad_probs - inner)).astype(BF16)
        grad_q = product(grad_scores, keys) * scaling
        dq_ref[:, lanes] = jnp.where(first, grad_q[:block], grad_q[block:]).astype(BF16)
        dk_acc[window, lanes] += dot_tn(grad_scores, queries)
        dv_acc[window, lanes] += dot_tn(probs.astype(BF16), grads)

    @pl.when(index == pl.num_programs(0) - 1)
    def _():
        dk_ref[...] = dk_acc[...].astype(BF16)
        dv_ref[...] = dv_acc[...].astype(BF16)


def attention_specs(length, columns):
    block = LANES
    width = min(length // 4 + block, length)
    whole = pl.BlockSpec((length, columns), lambda i: (0, 0))
    rows = pl.BlockSpec((block, columns), lambda i: (i, 0))
    seg_col = pl.BlockSpec((block, 1), lambda i: (i, 0))
    seg_row = pl.BlockSpec((1, length), lambda i: (0, 0))
    return block, width, whole, rows, seg_col, seg_row


def attend_forward(queries, keys, values, seg_all):
    length, columns = queries.shape
    block, width, whole, rows, seg_col, seg_row = attention_specs(length, columns)
    work = length * width * columns
    return pl.pallas_call(
        functools.partial(attend_forward_kernel, block=block, width=width),
        grid=(length // block,),
        in_specs=[rows, whole, whole, seg_col, seg_row],
        out_specs=rows,
        out_shape=jax.ShapeDtypeStruct((length, columns), BF16),
        cost_estimate=pl.CostEstimate(
            flops=16 * work, bytes_accessed=8 * length * columns, transcendentals=work // DH
        ),
        name="attend_forward",
    )(queries, keys, values, seg_all.reshape(length, 1), seg_all.reshape(1, length))


def attend_backward(queries, keys, values, grads, seg_all):
    length, columns = queries.shape
    block, width, whole, rows, seg_col, seg_row = attention_specs(length, columns)
    work = length * width * columns
    shape = jax.ShapeDtypeStruct((length, columns), BF16)
    return pl.pallas_call(
        functools.partial(attend_backward_kernel, block=block, width=width),
        grid=(length // block,),
        in_specs=[rows, whole, whole, rows, seg_col, seg_row],
        out_specs=[rows, whole, whole],
        out_shape=[shape, shape, shape],
        scratch_shapes=[pltpu.VMEM((length, columns), F32), pltpu.VMEM((length, columns), F32)],
        cost_estimate=pl.CostEstimate(
            flops=40 * work, bytes_accessed=14 * length * columns, transcendentals=work // DH
        ),
        name="attend_backward",
    )(queries, keys, values, grads, seg_all.reshape(length, 1), seg_all.reshape(1, length))


def expansion(heads):
    rows = lax.broadcasted_iota(jnp.int32, (2 * LANES, RANKS * heads * DH), 0) % LANES
    cols = lax.broadcasted_iota(jnp.int32, (2 * LANES, RANKS * heads * DH), 1)
    rank, head = cols // (heads * DH), (cols % (heads * DH)) // DH
    in_k = heads * RQ + head * RK + rank - RQ
    in_v = heads * (RQ + RK) + head * RK + rank - RQ - RK
    source = jnp.where(
        rank < RQ, head * RQ + rank, jnp.where(rank < RQ + RK, in_k, in_v)
    )
    return (rows == source).astype(BF16)


def high_low(values):
    high = values.astype(BF16)
    return high, (values - high.astype(F32)).astype(BF16)


def doubled(factor, rank, first):
    pair = factor[:, (rank // 2) * LANES : (rank // 2 + 1) * LANES]
    turned = pltpu.roll(pair, DH, 1)
    return jnp.where(first, pair, turned) if rank % 2 == 0 else jnp.where(first, turned, pair)


GROUPS = ((0, RQ), (RQ, RK), (RQ + RK, RK))


def heads_forward_kernel(x_ref, gain_ref, w_ref, e_ref, f_ref, q_ref, k_ref, v_ref):
    normed = rms_norm(x_ref[...].astype(F32), gain_ref[...]).astype(BF16)
    factor = product(normed, w_ref[...])
    f_ref[...] = factor
    spread = jnp.concatenate(high_low(factor[:, NB:]), axis=1)
    rows, columns = q_ref.shape
    first = lax.broadcasted_iota(jnp.int32, (rows, LANES), 1) < DH
    for (base, ranks), out_ref in zip(GROUPS, (q_ref, k_ref, v_ref)):
        total = None
        for rank in range(base, base + ranks):
            left = product(spread, e_ref[:, rank * columns : (rank + 1) * columns])
            right = jnp.concatenate([doubled(factor, rank, first)] * (columns // LANES), axis=1)
            total = left * right if total is None else total + left * right
        out_ref[...] = (total * (1.0 / ranks)).astype(BF16)


def heads_backward_kernel(f_ref, e_ref, dq_ref, dk_ref, dv_ref, g_ref):
    factor = f_ref[...]
    spread = jnp.concatenate(high_low(factor[:, NB:]), axis=1)
    rows, columns = dq_ref.shape
    first = lax.broadcasted_iota(jnp.int32, (rows, LANES), 1) < DH
    left_total = jnp.zeros((rows, LANES), F32)
    folded = []
    for (base, ranks), grad_ref in zip(GROUPS, (dq_ref, dk_ref, dv_ref)):
        grad = grad_ref[...].astype(F32) * (1.0 / ranks)
        for rank in range(base, base + ranks):
            ones = e_ref[:, rank * columns : (rank + 1) * columns]
            weighted = product(spread, ones) * grad
            right_grad = weighted[:, :LANES]
            for chunk in range(1, columns // LANES):
                right_grad = right_grad + weighted[:, chunk * LANES : (chunk + 1) * LANES]
            folded.append(right_grad + pltpu.roll(right_grad, DH, 1))
            right = jnp.concatenate([doubled(factor, rank, first)] * (columns // LANES), axis=1)
            high, low = high_low(grad * right)
            left_total = left_total + dot_nt(high, ones[:LANES]) + dot_nt(low, ones[:LANES])
    for pair in range(RANKS // 2):
        g_ref[:, pair * LANES : (pair + 1) * LANES] = jnp.where(
            first, folded[2 * pair], folded[2 * pair + 1]
        ).astype(BF16)
    g_ref[:, NB:] = left_total.astype(BF16)


HEAD_ROWS = 256


def heads_forward(tokens, gain_row, weights, spreader, columns):
    length, width = tokens.shape
    rows = min(HEAD_ROWS, length)
    block = lambda n: pl.BlockSpec((rows, n), lambda i: (i, 0))
    fixed = lambda a: pl.BlockSpec(a.shape, lambda i: (0, 0))
    head = jax.ShapeDtypeStruct((length, columns), BF16)
    return pl.pallas_call(
        heads_forward_kernel,
        grid=(length // rows,),
        in_specs=[block(width), fixed(gain_row), fixed(weights), fixed(spreader)],
        out_specs=[block(NB + LANES)] + [block(columns)] * 3,
        out_shape=[jax.ShapeDtypeStruct((length, NB + LANES), F32), head, head, head],
        name="heads_forward",
    )(tokens, gain_row, weights, spreader)


def heads_backward(factors, spreader, grad_q, grad_k, grad_v):
    length, columns = grad_q.shape
    rows = min(HEAD_ROWS, length)
    block = lambda n: pl.BlockSpec((rows, n), lambda i: (i, 0))
    return pl.pallas_call(
        heads_backward_kernel,
        grid=(length // rows,),
        in_specs=[
            block(NB + LANES), pl.BlockSpec(spreader.shape, lambda i: (0, 0)),
            block(columns), block(columns), block(columns),
        ],
        out_specs=block(NB + LANES),
        out_shape=jax.ShapeDtypeStruct((length, NB + LANES), BF16),
        name="heads_backward",
    )(factors, spreader, grad_q, grad_k, grad_v)


MESH_ID = pl.DeviceIdType.MESH


def place(count):
    me = lax.axis_index("fsdp")
    line, side, core = me // 4, (me // 2) % 2, me % 2
    return me, line, side, core, count // 4


def spot(line, side, core):
    return (line * 2 + side) * 2 + core


def meet(peers):
    barrier = pltpu.get_barrier_semaphore()
    for peer in peers:
        pl.semaphore_signal(barrier, inc=1, device_id=peer, device_id_type=MESH_ID)
    pl.semaphore_wait(barrier, len(peers))


def halves(columns):
    rank = lax.axis_index("sp")
    half = columns // 2
    own = pl.ds(pl.multiple_of(rank * half, LANES), half)
    other = pl.ds(pl.multiple_of((1 - rank) * half, LANES), half)
    return {"sp": 1 - rank}, own, other


def gather_kernel(x_ref, o_ref, local_sem, send_sem, recv_sem, line_sem, mate_sem, *, count, split):
    me, line, side, core, lines = place(count)
    across = [{"fsdp": spot(lax.rem(line + s, lines), side, core)} for s in range(1, lines)]
    beside, partner = {"fsdp": spot(line, 1 - side, core)}, {"fsdp": spot(line, side, 1 - core)}
    if split:
        mate, span, _ = halves(x_ref.shape[1])
    else:
        mate, span = None, slice(None)
    meet(across + [beside, partner] + ([mate] if split else []))
    sends = []

    def copy(src, dst, slot, sem, peer):
        return pltpu.make_async_remote_copy(
            src_ref=src, dst_ref=dst, send_sem=send_sem.at[slot], recv_sem=sem,
            device_id=peer, device_id_type=MESH_ID,
        )

    def send(src, dst, sem, peer):
        made = copy(src, dst, len(sends), sem, peer)
        made.start()
        sends.append(made)

    def forward(src, shard, peer):
        send(src, o_ref.at[shard], recv_sem.at[shard], peer)

    def arrive(ref, sem):
        copy(ref, ref, 0, sem, partner).wait_recv()

    own = pltpu.make_async_copy(x_ref, o_ref.at[me], local_sem)
    own.start()
    for peer in across:
        send(x_ref.at[:, span], o_ref.at[me, :, span], line_sem.at[me], peer)
    forward(x_ref, me, beside)
    forward(x_ref, me, partner)
    sources = [lax.rem(line + lines - s, lines) for s in range(1, lines)]
    if split:
        for source in sources:
            shard = spot(source, side, core)
            part = o_ref.at[shard, :, span]
            arrive(part, line_sem.at[shard])
            send(part, part, mate_sem.at[shard], mate)
    for source in sources:
        shard = spot(source, side, core)
        arrive(o_ref.at[shard, :, span], (mate_sem if split else line_sem).at[shard])
        forward(o_ref.at[shard], shard, beside)
        forward(o_ref.at[shard], shard, partner)
    for source in [line] + sources:
        shard = spot(source, 1 - side, core)
        arrive(o_ref.at[shard], recv_sem.at[shard])
        forward(o_ref.at[shard], shard, partner)
    for source in [line] + sources:
        for which in (side, 1 - side):
            shard = spot(source, which, 1 - core)
            arrive(o_ref.at[shard], recv_sem.at[shard])
    own.wait()
    for made in sends:
        made.wait_send()


def gather_packed(values, count, shards):
    lines = count // 4
    split = shards == 2
    sems = lambda n: pltpu.SemaphoreType.DMA((n,))
    return pl.pallas_call(
        functools.partial(gather_kernel, count=count, split=split),
        out_shape=jax.ShapeDtypeStruct((count,) + values.shape, values.dtype),
        in_specs=[pl.BlockSpec(memory_space=pltpu.VMEM)],
        out_specs=pl.BlockSpec(memory_space=pltpu.VMEM),
        scratch_shapes=[
            pltpu.SemaphoreType.DMA, sems(5 * lines - 2 if split else 4 * lines - 1),
            sems(count), sems(count), sems(count),
        ],
        compiler_params=pltpu.CompilerParams(collective_id=0, has_side_effects=True),
        name="gather_packed",
    )(values)


def scatter_kernel(
    fac_ref, out_ref, rest_ref, gains_ref, o_ref, part, core_in, side_in, line_in, mine, sp_in,
    core_send, core_recv, side_send, side_recv, line_send, line_recv, sp_send, sp_recv,
    *, count, shards
):
    me, line, side, core, lines = place(count)
    rank = lax.axis_index("sp")
    rows = o_ref.shape[0]
    across = [{"fsdp": spot(lax.rem(line + s, lines), side, core)} for s in range(1, lines)]
    beside, partner = {"fsdp": spot(line, 1 - side, core)}, {"fsdp": spot(line, side, 1 - core)}
    others = [{"sp": lax.rem(rank + s, shards)} for s in range(1, shards)]
    meet(across + [beside, partner] + others)
    started = []

    def copy(src, dst, send_sem, recv_sem, peer):
        return pltpu.make_async_remote_copy(
            src_ref=src, dst_ref=dst, send_sem=send_sem, recv_sem=recv_sem,
            device_id=peer, device_id_type=MESH_ID,
        )

    def send(*args):
        made = copy(*args)
        made.start()
        started.append(made)

    def load(shard):
        begin = pl.multiple_of(shard * rows, rows)
        return jnp.concatenate(
            [ref[pl.ds(begin, rows), :] for ref in (fac_ref, out_ref, rest_ref)]
            + [gains_ref[shard]],
            axis=1,
        )

    def from_core(slot):
        copy(part.at[me], core_in.at[slot], core_send.at[slot], core_recv.at[slot], partner).wait_recv()
        return core_in[slot].astype(F32)

    def from_side(slot):
        copy(part.at[me], side_in.at[slot], side_send.at[slot], side_recv.at[slot], beside).wait_recv()
        return side_in[slot].astype(F32)

    targets = [lax.rem(line + s, lines) for s in range(1, lines)] + [line]
    for which in (1 - side, side):
        for target in targets:
            shard = spot(target, which, 1 - core)
            slot = target * 2 + which
            part[shard] = load(shard)
            send(part.at[shard], core_in.at[slot], core_send.at[slot], core_recv.at[slot], partner)
    for target in targets:
        shard = spot(target, 1 - side, core)
        part[shard] = (load(shard).astype(F32) + from_core(target * 2 + 1 - side)).astype(BF16)
        send(part.at[shard], side_in.at[target], side_send.at[target], side_recv.at[target], beside)

    def whole_sum(target):
        shard = spot(target, side, core)
        return load(shard).astype(F32) + from_core(target * 2 + side) + from_side(target)

    for s, target in enumerate(targets):
        total = whole_sum(target)
        if s < lines - 1:
            shard = spot(target, side, core)
            part[shard] = total.astype(BF16)
            send(part.at[shard], line_in.at[s], line_send.at[s], line_recv.at[s], across[s])
    for s in range(lines - 1):
        copy(part.at[me], line_in.at[s], line_send.at[s], line_recv.at[s], across[s]).wait_recv()
        total = total + line_in[s].astype(F32)
    mine[0] = total.astype(BF16)
    for s, peer in enumerate(others):
        send(mine.at[0], sp_in.at[s], sp_send.at[s], sp_recv.at[s], peer)
    total = mine[0].astype(F32)
    for s, peer in enumerate(others):
        copy(mine.at[0], sp_in.at[s], sp_send.at[s], sp_recv.at[s], peer).wait_recv()
        total = total + sp_in[s].astype(F32)
    o_ref[...] = total
    for made in started:
        made.wait_send()


def scatter_packed(grad_fac, grad_out, grad_rest, grad_gains, count, shards):
    rows = grad_fac.shape[0] // count
    columns = sum(a.shape[-1] for a in (grad_fac, grad_out, grad_rest, grad_gains))
    lines = count // 4
    buffer = lambda n: pltpu.VMEM((n, rows, columns), BF16)
    sems = lambda n: pltpu.SemaphoreType.DMA((n,))
    return pl.pallas_call(
        functools.partial(scatter_kernel, count=count, shards=shards),
        out_shape=jax.ShapeDtypeStruct((rows, columns), F32),
        in_specs=[pl.BlockSpec(memory_space=pltpu.VMEM)] * 4,
        out_specs=pl.BlockSpec(memory_space=pltpu.VMEM),
        scratch_shapes=[
            buffer(count), buffer(2 * lines), buffer(lines), buffer(lines - 1),
            buffer(1), buffer(shards - 1),
            sems(2 * lines), sems(2 * lines), sems(lines), sems(lines),
            sems(lines - 1), sems(lines - 1), sems(shards - 1), sems(shards - 1),
        ],
        compiler_params=pltpu.CompilerParams(collective_id=1, has_side_effects=True),
        name="scatter_packed",
    )(grad_fac, grad_out, grad_rest, grad_gains)


def gather_shards(values, shards):
    me = lax.axis_index("sp")
    rows = values.shape[0]
    full = jnp.zeros((rows * shards,) + values.shape[1:], values.dtype)
    zeros = (0,) * (values.ndim - 1)
    full = lax.dynamic_update_slice(full, values, (me * rows,) + zeros)
    for shift in range(1, shards):
        part = lax.ppermute(values, "sp", [(i, (i + shift) % shards) for i in range(shards)])
        full = lax.dynamic_update_slice(full, part, (((me - shift) % shards) * rows,) + zeros)
    return full


def sum_shards(values, shards):
    if shards == 2:
        other = lax.ppermute(values, "sp", [(0, 1), (1, 0)])
        return values.astype(F32) + other.astype(F32)
    return lax.psum(values, "sp").astype(F32)


def arrange_factor(w, shards):
    heads = H // shards
    spans = ((0, RQ), (H * RQ, RK), (H * (RQ + RK), RK))
    parts = [w[:, H * RANKS :]]
    for device in range(shards):
        own = [
            w[:, base + device * heads * r : base + (device + 1) * heads * r] for base, r in spans
        ]
        parts.append(jnp.pad(jnp.concatenate(own, axis=1), ((0, 0), (0, LANES - heads * RANKS))))
    return jnp.concatenate(parts, axis=1)


def restore_factor(g, shards):
    heads = H // shards
    spans = ((0, RQ), (heads * RQ, RK), (heads * (RQ + RK), RK))
    parts = []
    for base, r in spans:
        for device in range(shards):
            begin = NB + device * LANES + base
            parts.append(g[:, begin : begin + heads * r])
    parts.append(g[:, :NB])
    return jnp.concatenate(parts, axis=1)


def local(tokens, segments, cotangent, gain_attn, w_fac, w_out, gain_ffn, w_gu, w_down, shards, count):
    me = lax.axis_index("sp")
    features = tokens.shape[2]
    heads = H // shards
    columns = heads * DH
    fac_columns = NB + shards * LANES
    own_rows = w_fac.shape[0]

    gains = jnp.concatenate([gain_attn, gain_ffn])[None]
    gains = jnp.pad(gains, ((0, own_rows - 1), (0, LANES - 2 * own_rows)))
    packed = jnp.concatenate([arrange_factor(w_fac, shards), w_out, gains], axis=1)
    packed = gather_packed(packed, count, shards)
    gu_full = lax.all_gather(w_gu, "fsdp", axis=0, tiled=True)
    down_full = lax.all_gather(w_down, "fsdp", axis=0, tiled=True)
    gains = packed[:, 0, fac_columns + features :].astype(F32)
    gain_one = gains[:, :own_rows].reshape(1, features)
    gain_two = gains[:, own_rows : 2 * own_rows].reshape(1, features)
    packed = packed.reshape(features, packed.shape[2])
    fac_full = packed[:, :fac_columns]
    out_full = packed[:, fac_columns : fac_columns + features]

    tokens_all = gather_shards(tokens[0], shards)
    seg_all = gather_shards(segments[0], shards)
    own_left = lax.dynamic_slice_in_dim(fac_full, NB + me * LANES, LANES, 1)
    own_weights = jnp.concatenate([fac_full[:, :NB], own_left], axis=1)
    spreader = expansion(heads)
    factors, query_heads, key_heads, value_heads = heads_forward(
        tokens_all, gain_one, own_weights, spreader, columns
    )
    mixed_heads = attend_forward(query_heads, key_heads, value_heads, seg_all)
    mixed_tokens = lax.all_to_all(mixed_heads, "sp", split_axis=0, concat_axis=1, tiled=True)

    inputs = tokens[0].astype(F32)
    token_count = inputs.shape[0]
    hidden_in = inputs + product(mixed_tokens, out_full)
    normed_two = rms_norm(hidden_in, gain_two).astype(BF16)
    gate_up = product(normed_two, gu_full)
    activated = swiglu(gate_up).astype(BF16)
    gate_up, activated = lax.optimization_barrier((gate_up, activated))
    grad_out = cotangent[0].astype(F32)
    grad_low = cotangent[0]
    grad_down = weight_grad(activated, grad_low).astype(BF16)
    grad_down = lax.psum_scatter(grad_down, "fsdp", scatter_dimension=0, tiled=True)

    result = hidden_in + product(activated, down_full)
    output = result.astype(BF16)[None]

    grad_act = back_product(grad_low, down_full)
    _, pull_ffn = jax.vjp(swiglu, gate_up)
    grad_gate_up = pull_ffn(grad_act)[0].astype(BF16)
    grad_normed_two = back_product(grad_gate_up, gu_full)
    _, pull_two = jax.vjp(rms_norm, hidden_in, gain_two)
    grad_from_norm, grad_gain_two = pull_two(grad_normed_two)
    grad_hidden = grad_out + grad_from_norm
    grad_branch = grad_hidden.astype(BF16)
    grad_mixed = back_product(grad_branch, out_full).astype(BF16)
    grad_gate_up, grad_mixed = lax.optimization_barrier((grad_gate_up, grad_mixed))
    kept = grad_gate_up.shape[1] - MOVED
    grad_gu = weight_grad(normed_two, grad_gate_up[:, :kept]).astype(BF16)
    grad_gu = lax.psum_scatter(grad_gu, "fsdp", scatter_dimension=0, tiled=True)
    grad_heads = lax.all_to_all(grad_mixed, "sp", split_axis=1, concat_axis=0, tiled=True)
    grad_q, grad_k, grad_v = attend_backward(
        query_heads, key_heads, value_heads, grad_heads, seg_all
    )
    grad_parts = heads_backward(factors, spreader, grad_q, grad_k, grad_v)
    grad_gate_up, grad_branch, grad_parts = lax.optimization_barrier(
        (grad_gate_up, grad_branch, grad_parts)
    )
    grad_rest = weight_grad(normed_two, grad_gate_up[:, kept:]).astype(BF16)
    grad_wout = weight_grad(mixed_tokens, grad_branch)
    grad_parts = lax.all_to_all(
        grad_parts.reshape(shards, token_count, NB + LANES), "sp", split_axis=0, concat_axis=0
    )
    grad_right = jnp.sum(grad_parts[:, :, :NB].astype(F32), axis=0).astype(BF16)
    grad_factor = jnp.concatenate(
        [grad_right] + [grad_parts[device, :, NB:] for device in range(shards)], axis=1
    )
    normed_one = rms_norm(inputs, gain_one).astype(BF16)
    grad_fac = weight_grad(normed_one, grad_factor)
    grad_normed_one = back_product(grad_factor, fac_full)
    _, pull_one = jax.vjp(rms_norm, inputs, gain_one)
    grad_in_norm, grad_gain_one = pull_one(grad_normed_one)
    grad_tokens = (grad_hidden + grad_in_norm).reshape(1, token_count, features)

    grad_gains = jnp.concatenate(
        [grad_gain_one.reshape(count, own_rows), grad_gain_two.reshape(count, own_rows)], axis=1
    )
    grad_gains = jnp.pad(
        grad_gains[:, None], ((0, 0), (0, own_rows - 1), (0, LANES - 2 * own_rows))
    )
    grad_packed = scatter_packed(
        grad_fac.astype(BF16), grad_wout.astype(BF16), grad_rest, grad_gains.astype(BF16),
        count, shards,
    )
    grad_down = sum_shards(grad_down, shards)
    grad_gu = sum_shards(grad_gu, shards)
    tail = fac_columns + features
    gain_row = grad_packed[0, tail + MOVED :]
    grad_gu = jnp.concatenate([grad_gu, grad_packed[:, tail : tail + MOVED]], axis=1)
    return (
        output,
        grad_tokens,
        gain_row[:own_rows],
        restore_factor(grad_packed[:, :fac_columns], shards),
        grad_packed[:, fac_columns : fac_columns + features],
        gain_row[own_rows : 2 * own_rows],
        grad_gu,
        grad_down,
    )


def solution(mesh):
    in_specs = (
        P("fsdp", "sp", None),
        P("fsdp", "sp"),
        P("fsdp", "sp", None),
        P("fsdp"),
        P("fsdp", None),
        P("fsdp", None),
        P("fsdp"),
        P("fsdp", None),
        P("fsdp", None),
    )
    out_specs = (
        P("fsdp", "sp", None),
        P("fsdp", "sp", None),
        P("fsdp"),
        P("fsdp", None),
        P("fsdp", None),
        P("fsdp"),
        P("fsdp", None),
        P("fsdp", None),
    )

    def body(*args):
        return local(*args, shards=mesh.shape["sp"], count=mesh.shape["fsdp"])

    return jax.shard_map(body, mesh=mesh, in_specs=in_specs, out_specs=out_specs, check_vma=False)
```
